512 devices in a mesh: wide: 64 (over z, x, core), narrow: 8 (over y).
Axes of the slice: x: 4, y: 8, z: 8, core: 2. Of those that a mesh axis runs over, the one named last changes fastest.
Arguments:
- charges: float32 [64, 1048576], P(None, ('wide', 'narrow')), may hold values from -6 to 6
- leaf_angle: float32 [64, 65536], P(None, ('wide', 'narrow')), may hold values from -3.140625 to 3.140625
- lagrange: float32 [48, 64], replicated, may hold values from -0.75 to 0.75
- level_angle: float32 [2, 48, 65536], P(None, None, ('wide', 'narrow')), may hold values from -3.140625 to 3.140625
- level_self: float32 [2, 96, 96], replicated, may hold values from -0.4375 to 0.4375
- level_peer: float32 [2, 96, 96], replicated, may hold values from -0.4375 to 0.4375
- switch_angle: float32 [48, 65536], P(None, ('wide', 'narrow')), may hold values from -3.140625 to 3.140625
- switch_matrix: float32 [96, 96], replicated, may hold values from -0.625 to 0.625
- out_angle: float32 [64, 65536], P(None, ('wide', 'narrow')), may hold values from -3.140625 to 3.140625
- evaluate: float32 [64, 48], replicated, may hold values from -0.875 to 0.875
Outputs:
- field: bfloat16 [64, 1048576], P(None, ('wide', 'narrow'))
The draws below stay inside these ranges and needn't reach their ends.
All inputs are finite; a program needn't handle non-finite values.
Results may differ from the reference program's by a relative error of at most 0.0049.
Values may be sent and summed in bfloat16 or wider, within the bound.
No kernel may reach another device: no remote copies, remote signals or barrier semaphores. Data moves between devices by JAX's collectives and lax.ppermute only.
A program may use at most 64 MiB of HBM per device.

```python
import jax
import jax.numpy as jnp
from jax import lax

K = 48
NRHS = 16
Q = 64
BOXES = 65536
COLUMNS = 1048576
N_WIDE = 64
N_NARROW = 8


def level_of(stream_key, dims, shards, least, largest):
    gain, own = 1.0, jax.random.fold_in(stream_key, 6)
    for dim, blocks in shards:
        heights = jnp.exp(jax.random.uniform(jax.random.fold_in(own, dim), (blocks,), jnp.float32, least / len(shards), largest / len(shards)))
        gain = gain * jnp.repeat(heights, dims[dim] // blocks).reshape([-1 if axis == dim else 1 for axis in range(len(dims))])
    return gain


def scatter_about(key, extent, spread, bound, split=(), held_as=jnp.bfloat16):
    drawn = spread * jax.random.normal(key, extent, jnp.float32)
    if split:
        drawn = drawn * level_of(key, extent, split, -0.22, 0.18)
    return jnp.clip(drawn, -bound, bound).astype(held_as)


def setup_inputs(seed: int = 0) -> dict:
    keys = jax.random.split(jax.random.key(seed), 11)
    return {
        "charges": scatter_about(keys[0], (Q, COLUMNS), 1.0, 6.0, ((1, 512),), jnp.float32),
        "leaf_angle": jnp.clip(jax.random.uniform(keys[1], (Q, BOXES), jnp.float32, -3.140625, 3.140625), -3.140625, 3.140625),
        "lagrange": scatter_about(keys[2], (K, Q), Q ** -0.5, 0.75, (), jnp.float32),
        "level_angle": jnp.clip(jax.random.uniform(keys[3], (2, K, BOXES), jnp.float32, -3.140625, 3.140625), -3.140625, 3.140625),
        "level_self": scatter_about(keys[4], (2, 2 * K, 2 * K), (4 * K) ** -0.5, 0.4375, (), jnp.float32),
        "level_peer": scatter_about(keys[5], (2, 2 * K, 2 * K), (4 * K) ** -0.5, 0.4375, (), jnp.float32),
        "switch_angle": jnp.clip(jax.random.uniform(keys[6], (K, BOXES), jnp.float32, -3.140625, 3.140625), -3.140625, 3.140625),
        "switch_matrix": scatter_about(keys[7], (2 * K, 2 * K), (2 * K) ** -0.5, 0.625, (), jnp.float32),
        "out_angle": jnp.clip(jax.random.uniform(keys[8], (Q, BOXES), jnp.float32, -3.140625, 3.140625), -3.140625, 3.140625),
        "evaluate": scatter_about(keys[9], (Q, K), K ** -0.5, 0.875, (), jnp.float32),
    }


def product(left, right):
    return jnp.dot(left, right, precision=lax.Precision.HIGHEST, preferred_element_type=jnp.float32)


def rotate(boxes_state, phase_angle, per_box):
    rank = phase_angle.shape[0]
    cos_part = jnp.repeat(jnp.cos(phase_angle), per_box, axis=1)
    sin_part = jnp.repeat(jnp.sin(phase_angle), per_box, axis=1)
    real_part = boxes_state[:rank]
    imag_part = boxes_state[rank:]
    return jnp.concatenate([cos_part * real_part - sin_part * imag_part, sin_part * real_part + cos_part * imag_part], axis=0)


def partner_state(boxes_state, bit):
    rows = boxes_state.shape[0]
    view = boxes_state.reshape(rows, N_WIDE, N_NARROW >> (bit + 1), 2, 1 << bit, -1)
    return jnp.flip(view, 3).reshape(boxes_state.shape)


def butterfly_level(boxes_state, self_matrix, peer_matrix, phase_angle, bit, per_box):
    rounded = lax.optimization_barrier(partner_state(boxes_state, bit).astype(jnp.bfloat16))
    combined = product(self_matrix, boxes_state) + product(peer_matrix, rounded.astype(jnp.float32))
    return rotate(combined, phase_angle, per_box)


def reference(charges, leaf_angle, lagrange, level_angle, level_self, level_peer, switch_angle, switch_matrix, out_angle, evaluate):
    per_box = NRHS
    rank = lagrange.shape[0]
    cos_leaf = jnp.repeat(jnp.cos(leaf_angle), per_box, axis=1)
    sin_leaf = jnp.repeat(jnp.sin(leaf_angle), per_box, axis=1)
    boxes_state = jnp.concatenate([product(lagrange, cos_leaf * charges), product(lagrange, sin_leaf * charges)], axis=0)
    boxes_state = butterfly_level(boxes_state, level_self[0], level_peer[0], level_angle[0], 0, per_box)
    rows = boxes_state.shape[0]
    view = boxes_state.reshape(rows, N_WIDE, N_NARROW, N_WIDE, -1)
    boxes_state = jnp.transpose(view, (0, 3, 2, 1, 4)).reshape(rows, -1)
    boxes_state = rotate(product(switch_matrix, boxes_state), switch_angle, per_box)
    last_bit = N_NARROW.bit_length() - 2
    boxes_state = butterfly_level(boxes_state, level_self[1], level_peer[1], level_angle[1], last_bit, per_box)
    real_part = product(evaluate, boxes_state[:rank])
    imag_part = product(evaluate, boxes_state[rank:])
    cos_out = jnp.repeat(jnp.cos(out_angle), per_box, axis=1)
    sin_out = jnp.repeat(jnp.sin(out_angle), per_box, axis=1)
    return (cos_out * real_part - sin_out * imag_part).astype(jnp.bfloat16)
```

```python
import jax
import jax.numpy as jnp
from jax import lax
from jax.experimental import pallas as pl
from jax.experimental.pallas import tpu as pltpu
from jax.sharding import PartitionSpec as P

F32 = jnp.float32
BF16 = jnp.bfloat16
LANES = 128
CHUNK = 256


def sin_cos(angle):
    turns = jnp.floor(angle * 0.6366197723675814 + 0.5)
    rest = angle - turns * 1.5703125
    rest = rest - turns * 4.837512969970703125e-4
    rest = rest - turns * 7.549789948768648e-8
    square = rest * rest
    sine = rest + rest * square * (
        -1.6666654611e-1 + square * (8.3321608736e-3 + square * -1.9515295891e-4)
    )
    cosine = (
        1.0
        - 0.5 * square
        + square
        * square
        * (4.166664568298827e-2 + square * (-1.388731625493765e-3 + square * 2.443315711809948e-5))
    )
    size = jnp.abs(turns)
    odd = size == 1.0
    sign = jnp.where(size == 2.0, -1.0, 1.0)
    return (
        jnp.where(odd, turns * cosine, sign * sine),
        jnp.where(odd, -turns * sine, sign * cosine),
    )


def halves(value):
    high = value.astype(BF16)
    return high, (value - high.astype(F32)).astype(BF16)


def dot(left, right):
    return jnp.dot(left, right, preferred_element_type=F32)


def dot_full(left, right, dims=((1,), (0,))):
    return lax.dot_general(
        left, right, (dims, ((), ())), precision=lax.Precision.HIGHEST, preferred_element_type=F32
    )


def spread(rows, scratch):
    scratch[...] = jnp.zeros((LANES, LANES), F32)
    for to_row, from_row in ((0, 0), (64, 48)):
        for to_lane, from_lane in ((0, 0), (64, 48)):
            scratch[to_row : to_row + 48, to_lane : to_lane + 48] = rows[
                from_row : from_row + 48, from_lane : from_lane + 48
            ]
    return scratch[...]


def two_blocks(block, scratch):
    scratch[...] = jnp.zeros((LANES, LANES), F32)
    scratch[0:48, 0:64] = block
    scratch[64:112, 64:128] = block
    return scratch[...]


def rotation_factors(angle):
    sine, cosine = sin_cos(angle)
    gap = jnp.zeros((16, LANES), F32)
    cos_rows = jnp.concatenate([cosine, gap, cosine, gap], axis=0)
    sin_rows = jnp.concatenate([-sine, gap, sine, gap], axis=0)
    return cos_rows.T, sin_rows.T


def per_box(value, factor):
    boxes = factor.shape[0]
    return (value.reshape(boxes, 16, LANES) * factor[:, None, :]).reshape(boxes * 16, LANES)


def rotated(value, cos_factor, sin_factor):
    return per_box(value, cos_factor) + per_box(pltpu.roll(value, 64, 1), sin_factor)


def pack_kernel(charges, leaf_angle, out):
    for tile in range(16):
        out[tile] = charges[:, tile * LANES : (tile + 1) * LANES].astype(BF16)
    high, low = halves(leaf_angle[...])
    out[16] = high
    out[17] = low


def source_part(read_tile, factors, weights_high, weights_low, emit):
    for chunk in range(2048 // CHUNK):
        rows = []
        for tile in range(chunk * CHUNK // LANES, (chunk + 1) * CHUNK // LANES):
            points = read_tile(tile)
            rows.append(jnp.concatenate([points, points], axis=0).T)
        value = jnp.concatenate(rows, axis=0)
        boxes = CHUNK // 16
        value = per_box(value, factors[chunk * boxes : (chunk + 1) * boxes, :])
        high, low = halves(value)
        emit(chunk, dot(high, weights_high) + dot(low, weights_high) + dot(high, weights_low))


def own_kernel(
    charges, leaf_angle, lagrange, level_angle, level_self, level_peer, own, weights, factors, scratch, turned
):
    leaf = two_blocks(lagrange[...], scratch)
    self_matrix = spread(level_self.at[0], scratch)
    own_weights = dot_full(leaf, self_matrix, ((0,), (1,)))
    peer_matrix = spread(level_peer.at[0], scratch)
    peer_weights = dot_full(leaf, peer_matrix, ((0,), (1,)))
    weights[0], weights[1] = halves(peer_weights)
    factors[0], factors[1] = rotation_factors(level_angle[0])
    sine, cosine = sin_cos(leaf_angle[...])
    turned[...] = jnp.concatenate([cosine, sine], axis=0).T
    own_high, own_low = halves(own_weights)

    def emit(chunk, value):
        own[chunk * CHUNK : (chunk + 1) * CHUNK, :] = value

    source_part(
        lambda tile: charges[:, tile * LANES : (tile + 1) * LANES], turned, own_high, own_low, emit
    )


def peer_kernel(received, own, weights, factors, out, turned):
    sine, cosine = sin_cos(received[16].astype(F32) + received[17].astype(F32))
    turned[...] = jnp.concatenate([cosine, sine], axis=0).T
    lane = lax.broadcasted_iota(jnp.int32, (CHUNK // 4, LANES), 1) % 64
    boxes = CHUNK // 16

    def emit(chunk, value):
        value = value + own[chunk * CHUNK : (chunk + 1) * CHUNK, :]
        value = rotated(
            value,
            factors[0, chunk * boxes : (chunk + 1) * boxes, :],
            factors[1, chunk * boxes : (chunk + 1) * boxes, :],
        )
        parts = value.reshape(CHUNK // 32, 4, 8, LANES)
        last = parts[:, 3].reshape(CHUNK // 4, LANES)
        packed = [
            jnp.where(lane < 48, parts[:, i].reshape(CHUNK // 4, LANES), pltpu.roll(last, shift, 1)).reshape(
                CHUNK // 32, 1, 8, LANES
            )
            for i, shift in enumerate((48, 32, 16))
        ]
        packed = jnp.concatenate(packed, axis=1).reshape(CHUNK * 3 // 4, LANES)
        out[chunk * CHUNK * 3 // 4 : (chunk + 1) * CHUNK * 3 // 4, :] = packed.astype(BF16)

    source_part(lambda tile: received[tile].astype(F32), turned, weights[0], weights[1], emit)


def target_kernel(
    level_angle, peer_angle, switch_angle, out_angle, level_self, level_peer, switch_matrix, evaluate, weights, factors, scratch
):
    weights[0], weights[1] = halves(spread(switch_matrix, scratch).T)
    weights[2], weights[3] = halves(spread(level_peer.at[1], scratch).T)
    weights[4], weights[5] = halves(spread(level_self.at[1], scratch).T)
    scratch[...] = jnp.zeros((LANES, LANES), F32)
    scratch[0:64, 0:48] = evaluate[...]
    scratch[64:128, 64:112] = evaluate[...]
    weights[6], weights[7] = halves(scratch[...].T)
    factors[0], factors[1] = rotation_factors(switch_angle[...])
    factors[2], factors[3] = rotation_factors(level_angle[1])
    sine, cosine = sin_cos(out_angle[...])
    factors[4] = jnp.concatenate([cosine, -sine], axis=0).T
    factors[5], factors[6] = rotation_factors(peer_angle[0:48])
    sine, cosine = sin_cos(peer_angle[48:112])
    factors[7] = jnp.concatenate([cosine, -sine], axis=0).T


def evaluated(value, cos_factor, sin_factor, out_factor, weights):
    value = rotated(value, cos_factor, sin_factor)
    high, low = halves(value)
    value = dot(high, weights[6]) + dot(low, weights[6]) + dot(high, weights[7])
    value = per_box(value, out_factor)
    tiles = []
    for tile in range(CHUNK // LANES):
        turned = value[tile * LANES : (tile + 1) * LANES, :].T
        tiles.append(turned[0:64] + turned[64:128])
    return jnp.concatenate(tiles, axis=1)


def switch_kernel(received, weights, factors, middle, sent):
    lane = lax.broadcasted_iota(jnp.int32, (CHUNK // 4, LANES), 1) % 64
    boxes = CHUNK // 16
    for chunk in range(2048 // CHUNK):
        packed = received[chunk * CHUNK * 3 // 4 : (chunk + 1) * CHUNK * 3 // 4, :].astype(F32)
        parts = packed.reshape(CHUNK // 32, 3, 8, LANES)
        first = [parts[:, i].reshape(CHUNK // 4, LANES) for i in range(3)]
        last = jnp.where(
            lane < 16,
            pltpu.roll(first[0], 80, 1),
            jnp.where(lane < 32, pltpu.roll(first[1], 96, 1), pltpu.roll(first[2], 112, 1)),
        )
        value = jnp.concatenate(
            [part.reshape(CHUNK // 32, 1, 8, LANES) for part in first + [last]], axis=1
        ).reshape(CHUNK, LANES)
        value = value.astype(BF16)
        value = dot(value, weights[0]) + dot(value, weights[1])
        here = pl.ds(chunk * boxes, boxes)
        value = rotated(value, factors[0, here, :], factors[1, here, :])
        middle[chunk * CHUNK : (chunk + 1) * CHUNK, :] = value
        value = value.astype(BF16)
        value = dot(value, weights[2]) + dot(value, weights[3])
        value = evaluated(value, factors[5, here, :], factors[6, here, :], factors[7, here, :], weights)
        sent[:, chunk * CHUNK : (chunk + 1) * CHUNK] = value.astype(BF16)


def last_kernel(middle, weights, factors, own):
    boxes = CHUNK // 16
    for chunk in range(2048 // CHUNK):
        high, low = halves(middle[chunk * CHUNK : (chunk + 1) * CHUNK, :])
        value = dot(high, weights[4]) + dot(low, weights[4]) + dot(high, weights[5])
        here = pl.ds(chunk * boxes, boxes)
        own[:, chunk * CHUNK : (chunk + 1) * CHUNK] = evaluated(
            value, factors[2, here, :], factors[3, here, :], factors[4, here, :], weights
        )


def add_kernel(own, received, out):
    out[...] = (own[...] + received[...].astype(F32)).astype(BF16)


def call(kernel, outs, args, scratch=(), name=None):
    whole = pl.BlockSpec(memory_space=pltpu.VMEM)
    shapes = [jax.ShapeDtypeStruct(shape, dtype) for shape, dtype in outs]
    return pl.pallas_call(
        kernel,
        out_shape=shapes if len(shapes) > 1 else shapes[0],
        in_specs=[whole] * len(args),
        out_specs=[whole] * len(shapes) if len(shapes) > 1 else whole,
        scratch_shapes=[pltpu.VMEM((LANES, LANES), F32)] * scratch if scratch else [],
        compiler_params=pltpu.CompilerParams(vmem_limit_bytes=32 * 1024 * 1024),
        name=name,
    )(*args)


def from_partner(value, apart):
    pairs = [(source, source ^ apart) for source in range(lax.axis_size("narrow"))]
    return lax.ppermute(value, "narrow", pairs)


def body(
    charges,
    leaf_angle,
    lagrange,
    level_angle,
    level_self,
    level_peer,
    switch_angle,
    switch_matrix,
    out_angle,
    evaluate,
):
    square = (LANES, LANES)
    packed = call(pack_kernel, [((18, 64, LANES), BF16)], [charges, leaf_angle], name="pack")
    near = from_partner(packed, 1)
    far_angle = from_partner(jnp.concatenate([level_angle[1], out_angle], axis=0), 4)
    own, weights, factors = call(
        own_kernel,
        [((2048, LANES), F32), ((2, *square), BF16), ((2, *square), F32)],
        [charges, leaf_angle, lagrange, level_angle, level_self, level_peer],
        2,
        name="own",
    )
    state = call(peer_kernel, [((1536, LANES), BF16)], [near, own, weights, factors], 1, name="peer")
    state = lax.all_to_all(state.reshape(64, 24, LANES), "wide", 0, 0, tiled=True).reshape(1536, LANES)
    weights, factors = call(
        target_kernel,
        [((8, *square), BF16), ((8, *square), F32)],
        [level_angle, far_angle, switch_angle, out_angle, level_self, level_peer, switch_matrix, evaluate],
        1,
        name="target",
    )
    middle, sent = call(
        switch_kernel,
        [((2048, LANES), F32), ((64, 2048), BF16)],
        [state, weights, factors],
        name="switch",
    )
    far = from_partner(sent, 4)
    own = call(last_kernel, [((64, 2048), F32)], [middle, weights, factors], name="last")
    return call(add_kernel, [((64, 2048), BF16)], [own, far], name="add")


def solution(mesh):
    return jax.shard_map(
        body,
        mesh=mesh,
        in_specs=(
            P(None, ("wide", "narrow")),
            P(None, ("wide", "narrow")),
            P(),
            P(None, None, ("wide", "narrow")),
            P(),
            P(),
            P(None, ("wide", "narrow")),
            P(),
            P(None, ("wide", "narrow")),
            P(),
        ),
        out_specs=P(None, ("wide", "narrow")),
        check_vma=False,
    )
```

```python
import jax
import jax.numpy as jnp
from jax import lax
from jax.experimental import pallas as pl
from jax.experimental.pallas import tpu as pltpu
from jax.sharding import PartitionSpec as P

F32 = jnp.float32
BF16 = jnp.bfloat16
LANES = 128
CHUNK = 256
WHOLE = 2048


def sin_cos(angle):
    turns = jnp.floor(angle * 0.6366197723675814 + 0.5)
    rest = angle - turns * 1.5703125
    rest = rest - turns * 4.837512969970703125e-4
    rest = rest - turns * 7.549789948768648e-8
    square = rest * rest
    sine = rest + rest * square * (
        -1.6666654611e-1 + square * (8.3321608736e-3 + square * -1.9515295891e-4)
    )
    cosine = (
        1.0
        - 0.5 * square
        + square
        * square
        * (4.166664568298827e-2 + square * (-1.388731625493765e-3 + square * 2.443315711809948e-5))
    )
    size = jnp.abs(turns)
    odd = size == 1.0
    sign = jnp.where(size == 2.0, -1.0, 1.0)
    return (
        jnp.where(odd, turns * cosine, sign * sine),
        jnp.where(odd, -turns * sine, sign * cosine),
    )


def halves(value):
    high = value.astype(BF16)
    return high, (value - high.astype(F32)).astype(BF16)


def dot(left, right):
    return jnp.dot(left, right, preferred_element_type=F32)


def dot_exact(value, weights):
    return dot(jnp.concatenate([value, value], axis=1), weights.reshape(2 * LANES, LANES))


def dot_wide(value, weights):
    high, low = halves(value)
    return dot_exact(high, weights) + dot(low, weights[0])


def dot_full(left, right, dims=((1,), (0,))):
    return lax.dot_general(
        left, right, (dims, ((), ())), precision=lax.Precision.HIGHEST, preferred_element_type=F32
    )


def spread(rows, scratch):
    scratch[...] = jnp.zeros((LANES, LANES), F32)
    for to_row, from_row in ((0, 0), (64, 48)):
        for to_lane, from_lane in ((0, 0), (64, 48)):
            scratch[to_row : to_row + 48, to_lane : to_lane + 48] = rows[
                from_row : from_row + 48, from_lane : from_lane + 48
            ]
    return scratch[...]


def two_blocks(block, scratch):
    scratch[...] = jnp.zeros((LANES, LANES), F32)
    scratch[0:48, 0:64] = block
    scratch[64:112, 64:128] = block
    return scratch[...]


def rotation_factors(angle):
    sine, cosine = sin_cos(angle)
    gap = jnp.zeros((16, LANES), F32)
    cos_rows = jnp.concatenate([cosine, gap, cosine, gap], axis=0)
    sin_rows = jnp.concatenate([-sine, gap, sine, gap], axis=0)
    return cos_rows.T, sin_rows.T


def per_box(value, factor):
    boxes = factor.shape[0]
    return (value.reshape(boxes, 16, LANES) * factor[:, None, :]).reshape(boxes * 16, LANES)


def rotated(value, cos_factor, sin_factor):
    return per_box(value, cos_factor) + per_box(pltpu.roll(value, 64, 1), sin_factor)


def pack_kernel(charges, leaf_angle, level_angle, out_angle, out, held, angle, far_angle, sems):
    width = 512
    copies = []
    for step in range(2048 // width):
        here = pl.ds(step * width, width)
        copies.append(pltpu.make_async_copy(charges.at[:, here], held.at[:, here], sems.at[step]))
    rest = [
        pltpu.make_async_copy(leaf_angle, angle, sems.at[4]),
        pltpu.make_async_copy(level_angle.at[1], far_angle.at[0:48], sems.at[5]),
        pltpu.make_async_copy(out_angle, far_angle.at[48:112], sems.at[6]),
    ]
    for copy in copies + rest:
        copy.start()
    for step, copy in enumerate(copies):
        copy.wait()
        for tile in range(step * width // LANES, (step + 1) * width // LANES):
            out[tile] = held[:, tile * LANES : (tile + 1) * LANES].astype(BF16)
    for copy in rest:
        copy.wait()
    high, low = halves(angle[...])
    out[16] = high
    out[17] = low


def source_part(read_tile, factors, weights, emit):
    for chunk in range(2048 // CHUNK):
        rows = []
        for tile in range(chunk * CHUNK // LANES, (chunk + 1) * CHUNK // LANES):
            points = read_tile(tile)
            rows.append(jnp.concatenate([points, points], axis=0).T)
        value = jnp.concatenate(rows, axis=0)
        boxes = CHUNK // 16
        value = per_box(value, factors[chunk * boxes : (chunk + 1) * boxes, :])
        emit(chunk, dot_wide(value, weights))


def own_kernel(
    charges, leaf_angle, lagrange, level_angle, level_self, level_peer, own, weights, factors, scratch, turned
):
    leaf = two_blocks(lagrange[...], scratch)
    self_matrix = spread(level_self.at[0], scratch)
    own_weights = dot_full(leaf, self_matrix, ((0,), (1,)))
    peer_matrix = spread(level_peer.at[0], scratch)
    peer_weights = dot_full(leaf, peer_matrix, ((0,), (1,)))
    weights[0], weights[1] = halves(peer_weights)
    factors[0], factors[1] = rotation_factors(level_angle[0])
    sine, cosine = sin_cos(leaf_angle[...])
    turned[...] = jnp.concatenate([cosine, sine], axis=0).T
    own_weights = jnp.stack(halves(own_weights))

    def emit(chunk, value):
        own[chunk * CHUNK : (chunk + 1) * CHUNK, :] = value

    source_part(
        lambda tile: charges[:, tile * LANES : (tile + 1) * LANES], turned, own_weights, emit
    )


def peer_kernel(received, own, weights, factors, out, turned):
    sine, cosine = sin_cos(received[16].astype(F32) + received[17].astype(F32))
    turned[...] = jnp.concatenate([cosine, sine], axis=0).T
    lane = lax.broadcasted_iota(jnp.int32, (CHUNK // 4, LANES), 1) % 64
    boxes = CHUNK // 16

    def emit(chunk, value):
        value = value + own[chunk * CHUNK : (chunk + 1) * CHUNK, :]
        value = rotated(
            value,
            factors[0, chunk * boxes : (chunk + 1) * boxes, :],
            factors[1, chunk * boxes : (chunk + 1) * boxes, :],
        )
        parts = value.reshape(CHUNK // 32, 4, 8, LANES)
        last = parts[:, 3].reshape(CHUNK // 4, LANES)
        packed = [
            jnp.where(lane < 48, parts[:, i].reshape(CHUNK // 4, LANES), pltpu.roll(last, shift, 1)).reshape(
                CHUNK // 32, 1, 8, LANES
            )
            for i, shift in enumerate((48, 32, 16))
        ]
        packed = jnp.concatenate(packed, axis=1).reshape(CHUNK * 3 // 4, LANES)
        out[chunk * CHUNK * 3 // 4 : (chunk + 1) * CHUNK * 3 // 4, :] = packed.astype(BF16)

    source_part(lambda tile: received[tile].astype(F32), turned, weights[...], emit)


def target_kernel(
    level_angle, peer_angle, switch_angle, out_angle, level_self, level_peer, switch_matrix, evaluate, weights, factors, scratch
):
    weights[0], weights[1] = halves(spread(switch_matrix, scratch).T)
    weights[2], weights[3] = halves(spread(level_peer.at[1], scratch).T)
    weights[4], weights[5] = halves(spread(level_self.at[1], scratch).T)
    scratch[...] = jnp.zeros((LANES, LANES), F32)
    scratch[0:64, 0:48] = evaluate[...]
    scratch[64:128, 64:112] = evaluate[...]
    weights[6], weights[7] = halves(scratch[...].T)
    factors[0], factors[1] = rotation_factors(switch_angle[...])
    factors[2], factors[3] = rotation_factors(level_angle[1])
    sine, cosine = sin_cos(out_angle[...])
    factors[4] = jnp.concatenate([cosine, -sine], axis=0).T
    factors[5], factors[6] = rotation_factors(peer_angle[0:48])
    sine, cosine = sin_cos(peer_angle[48:112])
    factors[7] = jnp.concatenate([cosine, -sine], axis=0).T


def evaluated(value, cos_factor, sin_factor, out_factor, weights):
    value = rotated(value, cos_factor, sin_factor)
    value = dot_wide(value, weights[6:8])
    value = per_box(value, out_factor)
    tiles = []
    for tile in range(value.shape[0] // LANES):
        turned = value[tile * LANES : (tile + 1) * LANES, :].T
        tiles.append(turned[0:64] + turned[64:128])
    return jnp.concatenate(tiles, axis=1)


def switch_kernel(received, weights, factors, middle, sent):
    lane = lax.broadcasted_iota(jnp.int32, (WHOLE // 4, LANES), 1) % 64
    boxes = WHOLE // 16
    for chunk in range(2048 // WHOLE):
        packed = received[chunk * WHOLE * 3 // 4 : (chunk + 1) * WHOLE * 3 // 4, :].astype(F32)
        parts = packed.reshape(WHOLE // 32, 3, 8, LANES)
        first = [parts[:, i].reshape(WHOLE // 4, LANES) for i in range(3)]
        last = jnp.where(
            lane < 16,
            pltpu.roll(first[0], 80, 1),
            jnp.where(lane < 32, pltpu.roll(first[1], 96, 1), pltpu.roll(first[2], 112, 1)),
        )
        value = jnp.concatenate(
            [part.reshape(WHOLE // 32, 1, 8, LANES) for part in first + [last]], axis=1
        ).reshape(WHOLE, LANES)
        value = value.astype(BF16)
        value = dot_exact(value, weights[0:2])
        here = pl.ds(chunk * boxes, boxes)
        value = rotated(value, factors[0, here, :], factors[1, here, :])
        middle[chunk * WHOLE : (chunk + 1) * WHOLE, :] = value
        value = value.astype(BF16)
        value = dot_exact(value, weights[2:4])
        value = evaluated(value, factors[5, here, :], factors[6, here, :], factors[7, here, :], weights)
        sent[:, chunk * WHOLE : (chunk + 1) * WHOLE] = value.astype(BF16)


def last_kernel(middle, weights, factors, own):
    boxes = CHUNK // 16
    for chunk in range(2048 // CHUNK):
        value = dot_wide(middle[chunk * CHUNK : (chunk + 1) * CHUNK, :], weights[4:6])
        here = pl.ds(chunk * boxes, boxes)
        own[:, chunk * CHUNK : (chunk + 1) * CHUNK] = evaluated(
            value, factors[2, here, :], factors[3, here, :], factors[4, here, :], weights
        )


def add_kernel(own, received, out):
    out[...] = (own[...] + received[...].astype(F32)).astype(BF16)


def call(kernel, outs, args, scratch=(), name=None, hbm=False):
    whole = pl.BlockSpec(memory_space=pltpu.VMEM)
    source = pl.BlockSpec(memory_space=pltpu.HBM) if hbm else whole
    shapes = [jax.ShapeDtypeStruct(shape, dtype) for shape, dtype in outs]
    return pl.pallas_call(
        kernel,
        out_shape=shapes if len(shapes) > 1 else shapes[0],
        in_specs=[source] * len(args),
        out_specs=[whole] * len(shapes) if len(shapes) > 1 else whole,
        scratch_shapes=scratch,
        compiler_params=pltpu.CompilerParams(vmem_limit_bytes=32 * 1024 * 1024),
        name=name,
    )(*args)


def from_partner(value, apart):
    pairs = [(source, source ^ apart) for source in range(lax.axis_size("narrow"))]
    return lax.ppermute(value, "narrow", pairs)


def body(
    charges,
    leaf_angle,
    lagrange,
    level_angle,
    level_self,
    level_peer,
    switch_angle,
    switch_matrix,
    out_angle,
    evaluate,
):
    square = (LANES, LANES)
    tile = pltpu.VMEM(square, F32)
    packed, charges, leaf_angle, far_angle = call(
        pack_kernel,
        [((18, 64, LANES), BF16), ((64, 2048), F32), ((64, LANES), F32), ((112, LANES), F32)],
        [pltpu.with_memory_space_constraint(x, pltpu.HBM) for x in (charges, leaf_angle, level_angle, out_angle)],
        [pltpu.SemaphoreType.DMA((7,))],
        name="pack",
        hbm=True,
    )
    near = from_partner(packed, 1)
    far_angle = from_partner(far_angle, 4)
    own, weights, factors = call(
        own_kernel,
        [((2048, LANES), F32), ((2, *square), BF16), ((2, *square), F32)],
        [charges, leaf_angle, lagrange, level_angle, level_self, level_peer],
        [tile] * 2,
        name="own",
    )
    near, far_angle = lax.optimization_barrier((near, far_angle))
    state = call(peer_kernel, [((1536, LANES), BF16)], [near, own, weights, factors], [tile], name="peer")
    state = lax.all_to_all(state.reshape(64, 24, LANES), "wide", 0, 0, tiled=True).reshape(1536, LANES)
    weights, factors = call(
        target_kernel,
        [((8, *square), BF16), ((8, *square), F32)],
        [level_angle, far_angle, switch_angle, out_angle, level_self, level_peer, switch_matrix, evaluate],
        [tile],
        name="target",
    )
    middle, sent = call(
        switch_kernel,
        [((2048, LANES), F32), ((64, 2048), BF16)],
        [state, weights, factors],
        name="switch",
    )
    far = from_partner(sent, 4)
    own = call(last_kernel, [((64, 2048), F32)], [middle, weights, factors], name="last")
    return call(add_kernel, [((64, 2048), BF16)], [own, far], name="add")


def solution(mesh):
    return jax.shard_map(
        body,
        mesh=mesh,
        in_specs=(
            P(None, ("wide", "narrow")),
            P(None, ("wide", "narrow")),
            P(),
            P(None, None, ("wide", "narrow")),
            P(),
            P(),
            P(None, ("wide", "narrow")),
            P(),
            P(None, ("wide", "narrow")),
            P(),
        ),
        out_specs=P(None, ("wide", "narrow")),
        check_vma=False,
    )
```

```python
import jax
import jax.numpy as jnp
from jax import lax
from jax.experimental import pallas as pl
from jax.experimental.pallas import tpu as pltpu
from jax.sharding import PartitionSpec as P

F32 = jnp.float32
BF16 = jnp.bfloat16
LANES = 128
CHUNK = 1024
WHOLE = 2048


def sin_cos(angle):
    turns = jnp.floor(angle * 0.6366197723675814 + 0.5)
    rest = angle - turns * 1.5703125
    rest = rest - turns * 4.837512969970703125e-4
    rest = rest - turns * 7.549789948768648e-8
    square = rest * rest
    sine = rest + rest * square * (
        -1.6666654611e-1 + square * (8.3321608736e-3 + square * -1.9515295891e-4)
    )
    cosine = (
        1.0
        - 0.5 * square
        + square
        * square
        * (4.166664568298827e-2 + square * (-1.388731625493765e-3 + square * 2.443315711809948e-5))
    )
    size = jnp.abs(turns)
    odd = size == 1.0
    sign = jnp.where(size == 2.0, -1.0, 1.0)
    return (
        jnp.where(odd, turns * cosine, sign * sine),
        jnp.where(odd, -turns * sine, sign * cosine),
    )


def halves(value):
    high = value.astype(BF16)
    return high, (value - high.astype(F32)).astype(BF16)


def dot(left, right):
    return jnp.dot(left, right, preferred_element_type=F32)


def wide_weights(matrix):
    high, low = halves(matrix)
    return jnp.concatenate(
        [jnp.concatenate([high, low], axis=1), jnp.concatenate([high, jnp.zeros_like(low)], axis=1)], axis=0
    )


def tall_weights(matrix):
    return jnp.concatenate(halves(matrix), axis=0)


def dot_exact(value, weights):
    return dot(jnp.concatenate([value, value], axis=1), weights)


def dot_wide(value, weights):
    both = dot(jnp.concatenate(halves(value), axis=1), weights)
    return both[:, :LANES] + both[:, LANES:]


def dot_full(left, right, dims=((1,), (0,))):
    return lax.dot_general(
        left, right, (dims, ((), ())), precision=lax.Precision.HIGHEST, preferred_element_type=F32
    )


def spread(rows, scratch):
    scratch[...] = jnp.zeros((LANES, LANES), F32)
    for to_row, from_row in ((0, 0), (64, 48)):
        for to_lane, from_lane in ((0, 0), (64, 48)):
            scratch[to_row : to_row + 48, to_lane : to_lane + 48] = rows[
                from_row : from_row + 48, from_lane : from_lane + 48
            ]
    return scratch[...]


def two_blocks(block, scratch):
    scratch[...] = jnp.zeros((LANES, LANES), F32)
    scratch[0:48, 0:64] = block
    scratch[64:112, 64:128] = block
    return scratch[...]


def rotation_factors(angle):
    sine, cosine = sin_cos(angle)
    gap = jnp.zeros((16, LANES), F32)
    cos_rows = jnp.concatenate([cosine, gap, cosine, gap], axis=0)
    sin_rows = jnp.concatenate([-sine, gap, sine, gap], axis=0)
    return cos_rows.T, sin_rows.T


def per_box(value, factor):
    boxes = factor.shape[0]
    return (value.reshape(boxes, 16, LANES) * factor[:, None, :]).reshape(boxes * 16, LANES)


def rotated(value, cos_factor, sin_factor):
    return per_box(value, cos_factor) + per_box(pltpu.roll(value, 64, 1), sin_factor)


def pack_kernel(charges, leaf_angle, level_angle, out_angle, out, held, angle, far_angle, sems):
    width = 512
    copies = []
    for step in range(2048 // width):
        here = pl.ds(step * width, width)
        copies.append(pltpu.make_async_copy(charges.at[:, here], held.at[:, here], sems.at[step]))
    rest = [
        pltpu.make_async_copy(leaf_angle, angle, sems.at[4]),
        pltpu.make_async_copy(level_angle.at[1], far_angle.at[0:48], sems.at[5]),
        pltpu.make_async_copy(out_angle, far_angle.at[48:112], sems.at[6]),
    ]
    for copy in copies + rest:
        copy.start()
    for step, copy in enumerate(copies):
        copy.wait()
        for tile in range(step * width // LANES, (step + 1) * width // LANES):
            out[tile] = held[:, tile * LANES : (tile + 1) * LANES].astype(BF16)
    for copy in rest:
        copy.wait()
    high, low = halves(angle[...])
    out[16] = high
    out[17] = low


def source_part(read_tile, factors, weights, emit):
    for chunk in range(2048 // CHUNK):
        rows = []
        for tile in range(chunk * CHUNK // LANES, (chunk + 1) * CHUNK // LANES):
            points = read_tile(tile)
            rows.append(jnp.concatenate([points, points], axis=0).T)
        value = jnp.concatenate(rows, axis=0)
        boxes = CHUNK // 16
        value = per_box(value, factors[chunk * boxes : (chunk + 1) * boxes, :])
        emit(chunk, dot_wide(value, weights))


def own_kernel(
    charges, leaf_angle, lagrange, level_angle, level_self, level_peer, own, weights, factors, scratch, turned
):
    leaf = two_blocks(lagrange[...], scratch)
    self_matrix = spread(level_self.at[0], scratch)
    own_weights = dot_full(leaf, self_matrix, ((0,), (1,)))
    peer_matrix = spread(level_peer.at[0], scratch)
    peer_weights = dot_full(leaf, peer_matrix, ((0,), (1,)))
    weights[...] = wide_weights(peer_weights)
    factors[0], factors[1] = rotation_factors(level_angle[0])
    sine, cosine = sin_cos(leaf_angle[...])
    turned[...] = jnp.concatenate([cosine, sine], axis=0).T
    own_weights = wide_weights(own_weights)

    def emit(chunk, value):
        own[chunk * CHUNK : (chunk + 1) * CHUNK, :] = value

    source_part(
        lambda tile: charges[:, tile * LANES : (tile + 1) * LANES], turned, own_weights, emit
    )


def peer_kernel(received, own, weights, factors, out, turned):
    sine, cosine = sin_cos(received[16].astype(F32) + received[17].astype(F32))
    turned[...] = jnp.concatenate([cosine, sine], axis=0).T
    lane = lax.broadcasted_iota(jnp.int32, (CHUNK // 4, LANES), 1) % 64
    boxes = CHUNK // 16

    def emit(chunk, value):
        value = value + own[chunk * CHUNK : (chunk + 1) * CHUNK, :]
        value = rotated(
            value,
            factors[0, chunk * boxes : (chunk + 1) * boxes, :],
            factors[1, chunk * boxes : (chunk + 1) * boxes, :],
        )
        parts = value.reshape(CHUNK // 32, 4, 8, LANES)
        last = parts[:, 3].reshape(CHUNK // 4, LANES)
        packed = [
            jnp.where(lane < 48, parts[:, i].reshape(CHUNK // 4, LANES), pltpu.roll(last, shift, 1)).reshape(
                CHUNK // 32, 1, 8, LANES
            )
            for i, shift in enumerate((48, 32, 16))
        ]
        packed = jnp.concatenate(packed, axis=1).reshape(CHUNK * 3 // 4, LANES)
        out[chunk * CHUNK * 3 // 4 : (chunk + 1) * CHUNK * 3 // 4, :] = packed.astype(BF16)

    source_part(lambda tile: received[tile].astype(F32), turned, weights[...], emit)


def target_kernel(
    level_angle, peer_angle, switch_angle, out_angle, level_self, level_peer, switch_matrix, evaluate, tall, wide, factors, scratch
):
    tall[0] = tall_weights(spread(switch_matrix, scratch).T)
    tall[1] = tall_weights(spread(level_peer.at[1], scratch).T)
    wide[0] = wide_weights(spread(level_self.at[1], scratch).T)
    scratch[...] = jnp.zeros((LANES, LANES), F32)
    scratch[0:64, 0:48] = evaluate[...]
    scratch[64:128, 64:112] = evaluate[...]
    wide[1] = wide_weights(scratch[...].T)
    factors[0], factors[1] = rotation_factors(switch_angle[...])
    factors[2], factors[3] = rotation_factors(level_angle[1])
    sine, cosine = sin_cos(out_angle[...])
    factors[4] = jnp.concatenate([cosine, -sine], axis=0).T
    factors[5], factors[6] = rotation_factors(peer_angle[0:48])
    sine, cosine = sin_cos(peer_angle[48:112])
    factors[7] = jnp.concatenate([cosine, -sine], axis=0).T


def evaluated(value, cos_factor, sin_factor, out_factor, last_weights):
    value = rotated(value, cos_factor, sin_factor)
    value = dot_wide(value, last_weights)
    value = per_box(value, out_factor)
    tiles = []
    for tile in range(value.shape[0] // LANES):
        turned = value[tile * LANES : (tile + 1) * LANES, :].T
        tiles.append(turned[0:64] + turned[64:128])
    return jnp.concatenate(tiles, axis=1)


def switch_kernel(received, tall, wide, factors, middle, sent):
    lane = lax.broadcasted_iota(jnp.int32, (WHOLE // 4, LANES), 1) % 64
    boxes = WHOLE // 16
    for chunk in range(2048 // WHOLE):
        packed = received[chunk * WHOLE * 3 // 4 : (chunk + 1) * WHOLE * 3 // 4, :].astype(F32)
        parts = packed.reshape(WHOLE // 32, 3, 8, LANES)
        first = [parts[:, i].reshape(WHOLE // 4, LANES) for i in range(3)]
        last = jnp.where(
            lane < 16,
            pltpu.roll(first[0], 80, 1),
            jnp.where(lane < 32, pltpu.roll(first[1], 96, 1), pltpu.roll(first[2], 112, 1)),
        )
        value = jnp.concatenate(
            [part.reshape(WHOLE // 32, 1, 8, LANES) for part in first + [last]], axis=1
        ).reshape(WHOLE, LANES)
        value = value.astype(BF16)
        value = dot_exact(value, tall[0])
        here = pl.ds(chunk * boxes, boxes)
        value = rotated(value, factors[0, here, :], factors[1, here, :])
        middle[chunk * WHOLE : (chunk + 1) * WHOLE, :] = value
        value = value.astype(BF16)
        value = dot_exact(value, tall[1])
        value = evaluated(value, factors[5, here, :], factors[6, here, :], factors[7, here, :], wide[1])
        sent[:, chunk * WHOLE : (chunk + 1) * WHOLE] = value.astype(BF16)


def last_kernel(middle, wide, factors, own):
    boxes = CHUNK // 16
    for chunk in range(2048 // CHUNK):
        value = dot_wide(middle[chunk * CHUNK : (chunk + 1) * CHUNK, :], wide[0])
        here = pl.ds(chunk * boxes, boxes)
        own[:, chunk * CHUNK : (chunk + 1) * CHUNK] = evaluated(
            value, factors[2, here, :], factors[3, here, :], factors[4, here, :], wide[1]
        )


def add_kernel(own, received, out):
    out[...] = (own[...] + received[...].astype(F32)).astype(BF16)


def call(kernel, outs, args, scratch=(), name=None, hbm=False):
    whole = pl.BlockSpec(memory_space=pltpu.VMEM)
    source = pl.BlockSpec(memory_space=pltpu.HBM) if hbm else whole
    shapes = [jax.ShapeDtypeStruct(shape, dtype) for shape, dtype in outs]
    return pl.pallas_call(
        kernel,
        out_shape=shapes if len(shapes) > 1 else shapes[0],
        in_specs=[source] * len(args),
        out_specs=[whole] * len(shapes) if len(shapes) > 1 else whole,
        scratch_shapes=scratch,
        compiler_params=pltpu.CompilerParams(vmem_limit_bytes=32 * 1024 * 1024),
        name=name,
    )(*args)


def from_partner(value, apart):
    pairs = [(source, source ^ apart) for source in range(lax.axis_size("narrow"))]
    return lax.ppermute(value, "narrow", pairs)


def body(
    charges,
    leaf_angle,
    lagrange,
    level_angle,
    level_self,
    level_peer,
    switch_angle,
    switch_matrix,
    out_angle,
    evaluate,
):
    square = (LANES, LANES)
    tile = pltpu.VMEM(square, F32)
    packed, charges, leaf_angle, far_angle = call(
        pack_kernel,
        [((18, 64, LANES), BF16), ((64, 2048), F32), ((64, LANES), F32), ((112, LANES), F32)],
        [pltpu.with_memory_space_constraint(x, pltpu.HBM) for x in (charges, leaf_angle, level_angle, out_angle)],
        [pltpu.SemaphoreType.DMA((7,))],
        name="pack",
        hbm=True,
    )
    near = from_partner(packed, 1)
    far_angle = from_partner(far_angle, 4)
    own, weights, factors = call(
        own_kernel,
        [((2048, LANES), F32), ((2 * LANES, 2 * LANES), BF16), ((2, *square), F32)],
        [charges, leaf_angle, lagrange, level_angle, level_self, level_peer],
        [tile] * 2,
        name="own",
    )
    state = call(peer_kernel, [((1536, LANES), BF16)], [near, own, weights, factors], [tile], name="peer")
    state = lax.all_to_all(state.reshape(64, 24, LANES), "wide", 0, 0, tiled=True).reshape(1536, LANES)
    tall, wide, factors = call(
        target_kernel,
        [((2, 2 * LANES, LANES), BF16), ((2, 2 * LANES, 2 * LANES), BF16), ((8, *square), F32)],
        [level_angle, far_angle, switch_angle, out_angle, level_self, level_peer, switch_matrix, evaluate],
        [tile],
        name="target",
    )
    middle, sent = call(
        switch_kernel,
        [((2048, LANES), F32), ((64, 2048), BF16)],
        [state, tall, wide, factors],
        name="switch",
    )
    far = from_partner(sent, 4)
    own = call(last_kernel, [((64, 2048), F32)], [middle, wide, factors], name="last")
    return call(add_kernel, [((64, 2048), BF16)], [own, far], name="add")


def solution(mesh):
    return jax.shard_map(
        body,
        mesh=mesh,
        in_specs=(
            P(None, ("wide", "narrow")),
            P(None, ("wide", "narrow")),
            P(),
            P(None, None, ("wide", "narrow")),
            P(),
            P(),
            P(None, ("wide", "narrow")),
            P(),
            P(None, ("wide", "narrow")),
            P(),
        ),
        out_specs=P(None, ("wide", "narrow")),
        check_vma=False,
    )
```

```python
import jax
import jax.numpy as jnp
from jax import lax
from jax.experimental import pallas as pl
from jax.experimental.pallas import tpu as pltpu
from jax.sharding import PartitionSpec as P

F32 = jnp.float32
BF16 = jnp.bfloat16
LANES = 128
CHUNK = 1024
WHOLE = 1024


def sin_cos(angle):
    turns = jnp.floor(angle * 0.6366197723675814 + 0.5)
    rest = angle - turns * 1.5703125
    rest = rest - turns * 4.837512969970703125e-4
    rest = rest - turns * 7.549789948768648e-8
    square = rest * rest
    sine = rest + rest * square * (
        -1.6666654611e-1 + square * (8.3321608736e-3 + square * -1.9515295891e-4)
    )
    cosine = (
        1.0
        - 0.5 * square
        + square
        * square
        * (4.166664568298827e-2 + square * (-1.388731625493765e-3 + square * 2.443315711809948e-5))
    )
    size = jnp.abs(turns)
    odd = size == 1.0
    sign = jnp.where(size == 2.0, -1.0, 1.0)
    return (
        jnp.where(odd, turns * cosine, sign * sine),
        jnp.where(odd, -turns * sine, sign * cosine),
    )


def halves(value):
    high = value.astype(BF16)
    return high, (value - high.astype(F32)).astype(BF16)


def dot(left, right):
    return jnp.dot(left, right, preferred_element_type=F32)


def wide_weights(matrix):
    high, low = halves(matrix)
    return jnp.concatenate(
        [jnp.concatenate([high, low], axis=1), jnp.concatenate([high, jnp.zeros_like(low)], axis=1)], axis=0
    )


def side_by_side(left, right, weights):
    both = dot(jnp.concatenate([left, right], axis=1), weights)
    return both[:, :LANES] + both[:, LANES:]


def dot_wide(value, weights):
    return side_by_side(*halves(value), weights)


def dot_full(left, right, dims=((1,), (0,))):
    return lax.dot_general(
        left, right, (dims, ((), ())), precision=lax.Precision.HIGHEST, preferred_element_type=F32
    )


def spread(rows, scratch):
    scratch[...] = jnp.zeros((LANES, LANES), F32)
    for to_row, from_row in ((0, 0), (64, 48)):
        for to_lane, from_lane in ((0, 0), (64, 48)):
            scratch[to_row : to_row + 48, to_lane : to_lane + 48] = rows[
                from_row : from_row + 48, from_lane : from_lane + 48
            ]
    return scratch[...]


def two_blocks(block, scratch):
    scratch[...] = jnp.zeros((LANES, LANES), F32)
    scratch[0:48, 0:64] = block
    scratch[64:112, 64:128] = block
    return scratch[...]


def rotation_factors(angle):
    sine, cosine = sin_cos(angle)
    gap = jnp.zeros((16, LANES), F32)
    cos_rows = jnp.concatenate([cosine, gap, cosine, gap], axis=0)
    sin_rows = jnp.concatenate([-sine, gap, sine, gap], axis=0)
    return cos_rows.T, sin_rows.T


def per_box(value, factor):
    boxes = factor.shape[0]
    return (value.reshape(boxes, 16, LANES) * factor[:, None, :]).reshape(boxes * 16, LANES)


def rotated(value, cos_factor, sin_factor):
    return per_box(value, cos_factor) + per_box(pltpu.roll(value, 64, 1), sin_factor)


def pack_kernel(charges, leaf_angle, out, held, angle, sems):
    width = 512
    copies = []
    for step in range(2048 // width):
        here = pl.ds(step * width, width)
        copies.append(pltpu.make_async_copy(charges.at[:, here], held.at[:, here], sems.at[step]))
    last = pltpu.make_async_copy(leaf_angle, angle, sems.at[4])
    for copy in copies + [last]:
        copy.start()
    for step, copy in enumerate(copies):
        copy.wait()
        for tile in range(step * width // LANES, (step + 1) * width // LANES):
            out[tile] = held[:, tile * LANES : (tile + 1) * LANES].astype(BF16)
    last.wait()
    high, low = halves(angle[...])
    out[16] = high
    out[17] = low


def source_part(read_tile, factors, weights, emit):
    for chunk in range(2048 // CHUNK):
        rows = []
        for tile in range(chunk * CHUNK // LANES, (chunk + 1) * CHUNK // LANES):
            points = read_tile(tile)
            rows.append(jnp.concatenate([points, points], axis=0).T)
        value = jnp.concatenate(rows, axis=0)
        boxes = CHUNK // 16
        value = per_box(value, factors[chunk * boxes : (chunk + 1) * boxes, :])
        emit(chunk, dot_wide(value, weights))


def own_kernel(
    charges, leaf_angle, lagrange, level_angle, level_self, level_peer, own, weights, factors, scratch, turned
):
    leaf = two_blocks(lagrange[...], scratch)
    self_matrix = spread(level_self.at[0], scratch)
    own_weights = dot_full(leaf, self_matrix, ((0,), (1,)))
    peer_matrix = spread(level_peer.at[0], scratch)
    peer_weights = dot_full(leaf, peer_matrix, ((0,), (1,)))
    weights[...] = wide_weights(peer_weights)
    factors[0], factors[1] = rotation_factors(level_angle[0])
    sine, cosine = sin_cos(leaf_angle[...])
    turned[...] = jnp.concatenate([cosine, sine], axis=0).T
    own_weights = wide_weights(own_weights)

    def emit(chunk, value):
        own[chunk * CHUNK : (chunk + 1) * CHUNK, :] = value

    source_part(
        lambda tile: charges[:, tile * LANES : (tile + 1) * LANES], turned, own_weights, emit
    )


def peer_kernel(received, own, weights, factors, out, turned):
    sine, cosine = sin_cos(received[16].astype(F32) + received[17].astype(F32))
    turned[...] = jnp.concatenate([cosine, sine], axis=0).T
    lane = lax.broadcasted_iota(jnp.int32, (CHUNK // 4, LANES), 1) % 64
    boxes = CHUNK // 16

    def emit(chunk, value):
        value = value + own[chunk * CHUNK : (chunk + 1) * CHUNK, :]
        value = rotated(
            value,
            factors[0, chunk * boxes : (chunk + 1) * boxes, :],
            factors[1, chunk * boxes : (chunk + 1) * boxes, :],
        )
        parts = value.reshape(CHUNK // 32, 4, 8, LANES)
        last = parts[:, 3].reshape(CHUNK // 4, LANES)
        packed = [
            jnp.where(lane < 48, parts[:, i].reshape(CHUNK // 4, LANES), pltpu.roll(last, shift, 1)).reshape(
                CHUNK // 32, 1, 8, LANES
            )
            for i, shift in enumerate((48, 32, 16))
        ]
        packed = jnp.concatenate(packed * 2, axis=1).reshape(CHUNK * 3 // 2, LANES)
        out[chunk * CHUNK * 3 // 2 : (chunk + 1) * CHUNK * 3 // 2, :] = packed.astype(BF16)

    source_part(lambda tile: received[tile].astype(F32), turned, weights[...], emit)


def target_kernel(
    side, level_angle, far_angle, switch_angle, out_angle, level_self, level_peer, switch_matrix, evaluate, switch_weights, level_weights, last_weights, factors, scratch
):
    first = side[0] == 0
    high, low = halves(spread(switch_matrix, scratch).T)
    switch_weights[...] = jnp.concatenate([high, low], axis=0)
    peer_matrix = spread(level_peer.at[1], scratch).T
    self_matrix = spread(level_self.at[1], scratch).T
    for place, matrix in enumerate((jnp.where(first, self_matrix, peer_matrix), jnp.where(first, peer_matrix, self_matrix))):
        high, low = halves(matrix)
        level_weights[place * LANES : (place + 1) * LANES, :] = jnp.concatenate([high, low], axis=1)
    scratch[...] = jnp.zeros((LANES, LANES), F32)
    scratch[0:64, 0:48] = evaluate[...]
    scratch[64:128, 64:112] = evaluate[...]
    last_weights[...] = wide_weights(scratch[...].T)
    here, there = switch_angle[...], far_angle[...]
    factors[0], factors[1] = rotation_factors(jnp.where(first, here, there))
    factors[2], factors[3] = rotation_factors(jnp.where(first, there, here))
    factors[4], factors[5] = rotation_factors(level_angle[1])
    sine, cosine = sin_cos(out_angle[...])
    factors[6] = jnp.concatenate([cosine, -sine], axis=0).T


def field_kernel(received, switch_weights, level_weights, last_weights, factors, out):
    lane = lax.broadcasted_iota(jnp.int32, (WHOLE // 4, LANES), 1) % 64
    boxes = WHOLE // 16
    for chunk in range(2048 // WHOLE):
        here = pl.ds(chunk * boxes, boxes)
        packed = received[chunk * WHOLE * 3 // 2 : (chunk + 1) * WHOLE * 3 // 2, :].astype(F32)
        parts = packed.reshape(WHOLE // 32, 6, 8, LANES)
        sides = []
        for side in range(2):
            first = [parts[:, 3 * side + i].reshape(WHOLE // 4, LANES) for i in range(3)]
            last = jnp.where(
                lane < 16,
                pltpu.roll(first[0], 80, 1),
                jnp.where(lane < 32, pltpu.roll(first[1], 96, 1), pltpu.roll(first[2], 112, 1)),
            )
            value = jnp.concatenate(
                [part.reshape(WHOLE // 32, 1, 8, LANES) for part in first + [last]], axis=1
            ).reshape(WHOLE, LANES)
            value = value.astype(BF16)
            value = dot(jnp.concatenate([value, value], axis=1), switch_weights[...])
            value = rotated(value, factors[2 * side, here, :], factors[2 * side + 1, here, :])
            sides.append(value.astype(BF16))
        value = side_by_side(*sides, level_weights[...])
        value = rotated(value, factors[4, here, :], factors[5, here, :])
        value = per_box(dot_wide(value, last_weights[...]), factors[6, here, :])
        for tile in range(WHOLE // LANES):
            turned = value[tile * LANES : (tile + 1) * LANES, :].T
            at = chunk * WHOLE + tile * LANES
            out[:, at : at + LANES] = (turned[0:64] + turned[64:128]).astype(BF16)


def call(kernel, outs, args, scratch=(), name=None, spaces=pltpu.VMEM):
    whole = pl.BlockSpec(memory_space=pltpu.VMEM)
    if not isinstance(spaces, list):
        spaces = [spaces] * len(args)
    shapes = [jax.ShapeDtypeStruct(shape, dtype) for shape, dtype in outs]
    return pl.pallas_call(
        kernel,
        out_shape=shapes if len(shapes) > 1 else shapes[0],
        in_specs=[pl.BlockSpec(memory_space=space) for space in spaces],
        out_specs=[whole] * len(shapes) if len(shapes) > 1 else whole,
        scratch_shapes=scratch,
        compiler_params=pltpu.CompilerParams(vmem_limit_bytes=32 * 1024 * 1024),
        name=name,
    )(*args)


def from_partner(value, apart):
    pairs = [(source, source ^ apart) for source in range(lax.axis_size("narrow"))]
    return lax.ppermute(value, "narrow", pairs)


def body(
    charges,
    leaf_angle,
    lagrange,
    level_angle,
    level_self,
    level_peer,
    switch_angle,
    switch_matrix,
    out_angle,
    evaluate,
):
    square = (LANES, LANES)
    tile = pltpu.VMEM(square, F32)
    wide, narrow = lax.axis_size("wide"), lax.axis_size("narrow")
    apart = narrow // 2
    packed, charges, leaf_angle = call(
        pack_kernel,
        [((18, 64, LANES), BF16), ((64, 2048), F32), ((64, LANES), F32)],
        [pltpu.with_memory_space_constraint(x, pltpu.HBM) for x in (charges, leaf_angle)],
        [pltpu.SemaphoreType.DMA((5,))],
        name="pack",
        spaces=pltpu.HBM,
    )
    near = from_partner(packed, 1)
    own, weights, factors = call(
        own_kernel,
        [((2048, LANES), F32), ((2 * LANES, 2 * LANES), BF16), ((2, *square), F32)],
        [charges, leaf_angle, lagrange, level_angle, level_self, level_peer],
        [tile] * 2,
        name="own",
    )
    state = call(peer_kernel, [((3072, LANES), BF16)], [near, own, weights, factors], [tile], name="peer")
    groups = [
        [w * narrow + r + apart * side for w in range(wide) for side in range(2)] for r in range(apart)
    ]
    state = lax.all_to_all(
        state.reshape(2 * wide, 24, LANES),
        ("wide", "narrow"),
        0,
        0,
        axis_index_groups=groups,
        tiled=True,
    ).reshape(3072, LANES)
    far_angle = from_partner(switch_angle, apart)
    side = (lax.axis_index("narrow") // apart).astype(jnp.int32).reshape(1)
    *weights, factors = call(
        target_kernel,
        [((2 * LANES, LANES), BF16), ((2 * LANES, 2 * LANES), BF16), ((2 * LANES, 2 * LANES), BF16), ((7, *square), F32)],
        [side, level_angle, far_angle, switch_angle, out_angle, level_self, level_peer, switch_matrix, evaluate],
        [tile],
        name="target",
        spaces=[pltpu.SMEM] + [pltpu.VMEM] * 8,
    )
    return call(field_kernel, [((64, 2048), BF16)], [state, *weights, factors], name="field")


def solution(mesh):
    return jax.shard_map(
        body,
        mesh=mesh,
        in_specs=(
            P(None, ("wide", "narrow")),
            P(None, ("wide", "narrow")),
            P(),
            P(None, None, ("wide", "narrow")),
            P(),
            P(),
            P(None, ("wide", "narrow")),
            P(),
            P(None, ("wide", "narrow")),
            P(),
        ),
        out_specs=P(None, ("wide", "narrow")),
        check_vma=False,
    )
```

```python
import jax
import jax.numpy as jnp
from jax import lax
from jax.experimental import pallas as pl
from jax.experimental.pallas import tpu as pltpu
from jax.sharding import PartitionSpec as P

F32 = jnp.float32
BF16 = jnp.bfloat16
LANES = 128
CHUNK = 1024
WHOLE = 2048


def sin_cos(angle):
    turns = jnp.floor(angle * 0.6366197723675814 + 0.5)
    rest = angle - turns * 1.5703125
    rest = rest - turns * 4.837512969970703125e-4
    rest = rest - turns * 7.549789948768648e-8
    square = rest * rest
    sine = rest + rest * square * (
        -1.6666654611e-1 + square * (8.3321608736e-3 + square * -1.9515295891e-4)
    )
    cosine = (
        1.0
        - 0.5 * square
        + square
        * square
        * (4.166664568298827e-2 + square * (-1.388731625493765e-3 + square * 2.443315711809948e-5))
    )
    size = jnp.abs(turns)
    odd = size == 1.0
    sign = jnp.where(size == 2.0, -1.0, 1.0)
    return (
        jnp.where(odd, turns * cosine, sign * sine),
        jnp.where(odd, -turns * sine, sign * cosine),
    )


def halves(value):
    high = value.astype(BF16)
    return high, (value - high.astype(F32)).astype(BF16)


def dot(left, right):
    return jnp.dot(left, right, preferred_element_type=F32)


def wide_weights(matrix):
    high, low = halves(matrix)
    return jnp.concatenate(
        [jnp.concatenate([high, low], axis=1), jnp.concatenate([high, jnp.zeros_like(low)], axis=1)], axis=0
    )


def tall_weights(matrix):
    return jnp.concatenate(halves(matrix), axis=0)


def dot_exact(value, weights):
    return dot(jnp.concatenate([value, value], axis=1), weights)


def dot_wide(value, weights):
    both = dot(jnp.concatenate(halves(value), axis=1), weights)
    return both[:, :LANES] + both[:, LANES:]


def dot_full(left, right, dims=((1,), (0,))):
    return lax.dot_general(
        left, right, (dims, ((), ())), precision=lax.Precision.HIGHEST, preferred_element_type=F32
    )


def spread(rows, scratch):
    scratch[...] = jnp.zeros((LANES, LANES), F32)
    for to_row, from_row in ((0, 0), (64, 48)):
        for to_lane, from_lane in ((0, 0), (64, 48)):
            scratch[to_row : to_row + 48, to_lane : to_lane + 48] = rows[
                from_row : from_row + 48, from_lane : from_lane + 48
            ]
    return scratch[...]


def two_blocks(block, scratch):
    scratch[...] = jnp.zeros((LANES, LANES), F32)
    scratch[0:48, 0:64] = block
    scratch[64:112, 64:128] = block
    return scratch[...]


def rotation_factors(angle):
    sine, cosine = sin_cos(angle)
    gap = jnp.zeros((16, LANES), F32)
    cos_rows = jnp.concatenate([cosine, gap, cosine, gap], axis=0)
    sin_rows = jnp.concatenate([-sine, gap, sine, gap], axis=0)
    return cos_rows.T, sin_rows.T


def per_box(value, factor):
    boxes = factor.shape[0]
    return (value.reshape(boxes, 16, LANES) * factor[:, None, :]).reshape(boxes * 16, LANES)


def rotated(value, cos_factor, sin_factor):
    return per_box(value, cos_factor) + per_box(pltpu.roll(value, 64, 1), sin_factor)


GROUP = 4
PIECE = 20


def piece_rows(backward):
    pieces = lax.broadcasted_iota(jnp.int32, (8 * PIECE, 8 * PIECE), 1 if backward else 0)
    rows = lax.broadcasted_iota(jnp.int32, (8 * PIECE, 8 * PIECE), 0 if backward else 1)
    place, row = pieces // PIECE, pieces % PIECE
    wide, side = place // 2, place % 2
    angle = row - 16
    found = jnp.where(row < 16, wide * 16 + row, 64 + (angle // 2) * 8 + wide * 2 + angle % 2)
    if backward:
        return (rows == side * 80 + found).astype(F32).astype(BF16)
    return (rows == found).astype(F32).astype(BF16)[:, :80]


def angle_rows(angle):
    high = angle.astype(BF16).astype(F32)
    low = angle - high
    if angle.shape[0] == 64:
        return jnp.concatenate([high, low], axis=0).T
    gap = jnp.zeros((16, LANES), F32)
    return jnp.concatenate([high, gap, low, gap], axis=0).T


def pack_kernel(charges, leaf_angle, level_angle, out_angle, out, far_angle, held, angle, first_angle, sems):
    width = 512
    copies = []
    for step in range(2048 // width):
        here = pl.ds(step * width, width)
        copies.append(pltpu.make_async_copy(charges.at[:, here], held.at[:, here], sems.at[step]))
    near = [
        pltpu.make_async_copy(leaf_angle, angle, sems.at[4]),
        pltpu.make_async_copy(level_angle.at[0], first_angle, sems.at[5]),
    ]
    far = [
        pltpu.make_async_copy(level_angle.at[1], far_angle.at[0:48], sems.at[6]),
        pltpu.make_async_copy(out_angle, far_angle.at[48:112], sems.at[7]),
    ]
    for copy in near + copies + far:
        copy.start()
    order = piece_rows(False)
    low_lane = lax.broadcasted_iota(jnp.int32, (64, LANES), 1) < 64
    for copy in near:
        copy.wait()
    leaf_rows = angle_rows(angle[...])
    level_rows = angle_rows(first_angle[...])
    for tile in range(16):
        if tile % 4 == 0:
            copies[tile // 4].wait()
        points = held[:, tile * LANES : (tile + 1) * LANES]
        both = jnp.concatenate([points, points], axis=0).T.reshape(GROUP, 2, 16, LANES)
        merged = jnp.where(low_lane, both[:, 0].reshape(64, LANES), both[:, 1].reshape(64, LANES))
        boxes = slice(tile * 8, (tile + 1) * 8)
        rows = jnp.concatenate([merged, leaf_rows[boxes], level_rows[boxes]], axis=0).astype(BF16)
        out[tile * 160 : (tile + 1) * 160, :] = dot(order, rows).astype(BF16)
    for copy in far:
        copy.wait()


def target_kernel(
    parity, lagrange, level_angle, peer_angle, switch_angle, out_angle, level_self, level_peer, switch_matrix, evaluate, source, tall, wide, factors, scratch
):
    leaf = two_blocks(lagrange[...], scratch)
    self_weights = dot_full(leaf, spread(level_self.at[0], scratch), ((0,), (1,)))
    peer_weights = dot_full(leaf, spread(level_peer.at[0], scratch), ((0,), (1,)))
    even = parity[0] == 0
    for place in range(2):
        near, far = (self_weights, peer_weights) if place == 0 else (peer_weights, self_weights)
        high, low = halves(jnp.where(even, near, far))
        source[place * LANES : (place + 1) * LANES, :] = jnp.concatenate([high, low], axis=1)
    tall[...] = tall_weights(spread(level_peer.at[1], scratch).T)
    wide[0] = wide_weights(spread(level_self.at[1], scratch).T)
    scratch[...] = jnp.zeros((LANES, LANES), F32)
    scratch[0:64, 0:48] = evaluate[...]
    scratch[64:128, 64:112] = evaluate[...]
    wide[1] = wide_weights(scratch[...].T)
    wide[2] = wide_weights(spread(switch_matrix, scratch).T)
    factors[0], factors[1] = rotation_factors(switch_angle[...])
    factors[2], factors[3] = rotation_factors(level_angle[1])
    sine, cosine = sin_cos(out_angle[...])
    factors[4] = jnp.concatenate([cosine, -sine], axis=0).T
    factors[5], factors[6] = rotation_factors(peer_angle[0:48])
    sine, cosine = sin_cos(peer_angle[48:112])
    factors[7] = jnp.concatenate([cosine, -sine], axis=0).T


def evaluated(value, cos_factor, sin_factor, out_factor, last_weights):
    value = rotated(value, cos_factor, sin_factor)
    value = dot_wide(value, last_weights)
    value = per_box(value, out_factor)
    tiles = []
    for tile in range(value.shape[0] // LANES):
        turned = value[tile * LANES : (tile + 1) * LANES, :].T
        tiles.append(turned[0:64] + turned[64:128])
    return jnp.concatenate(tiles, axis=1)


def switch_kernel(parity, received, source, tall, wide, factors, middle, sent, points, turns):
    order = piece_rows(True)
    low_lane = lax.broadcasted_iota(jnp.int32, (64, LANES), 1) < 64
    for group in range(16):
        rows = dot(order, received[group * 160 : (group + 1) * 160, :])
        for side in range(2):
            merged = rows[side * 80 : side * 80 + 64]
            exchanged = pltpu.roll(merged, 64, 1)
            pair = [
                jnp.where(low_lane, merged, exchanged).reshape(GROUP, 1, 16, LANES),
                jnp.where(low_lane, exchanged, merged).reshape(GROUP, 1, 16, LANES),
            ]
            points[side, group * LANES : (group + 1) * LANES, :] = jnp.concatenate(pair, axis=1).reshape(LANES, LANES)
            turns[side, group * 8 : (group + 1) * 8, :] = rows[side * 80 + 64 : side * 80 + 72]
            turns[2 + side, group * 8 : (group + 1) * 8, :] = rows[side * 80 + 72 : side * 80 + 80]
    first_half = lax.broadcasted_iota(jnp.int32, (LANES, LANES), 1) < 64
    for side in range(2):
        angle = turns[side] + pltpu.roll(turns[side], 64, 1)
        sine, cosine = sin_cos(angle)
        turns[side] = jnp.where(first_half, cosine, sine)
    angle = jnp.where(parity[0] == 0, turns[2], turns[3])
    sine, cosine = sin_cos(angle + pltpu.roll(angle, 64, 1))
    turns[2] = cosine
    turns[3] = jnp.where(first_half, -sine, sine)
    boxes = WHOLE // 16
    for chunk in range(2048 // WHOLE):
        here = pl.ds(chunk * boxes, boxes)
        there = pl.ds(chunk * WHOLE, WHOLE)
        parts = [halves(per_box(points[side, there, :], turns[side, here, :])) for side in range(2)]
        both = dot(jnp.concatenate([parts[0][0], parts[1][0]], axis=1), source[...])
        value = both[:, :LANES] + both[:, LANES:]
        value = value + dot(jnp.concatenate([parts[0][1], parts[1][1]], axis=1), source[:, :LANES])
        value = rotated(value, turns[2, here, :], turns[3, here, :])
        value = dot_wide(value, wide[2])
        value = rotated(value, factors[0, here, :], factors[1, here, :])
        middle[there, :] = value
        value = dot_exact(value.astype(BF16), tall[...])
        value = evaluated(value, factors[5, here, :], factors[6, here, :], factors[7, here, :], wide[1])
        sent[:, there] = value.astype(BF16)


def last_kernel(middle, wide, factors, own):
    boxes = CHUNK // 16
    for chunk in range(2048 // CHUNK):
        value = dot_wide(middle[chunk * CHUNK : (chunk + 1) * CHUNK, :], wide[0])
        here = pl.ds(chunk * boxes, boxes)
        own[:, chunk * CHUNK : (chunk + 1) * CHUNK] = evaluated(
            value, factors[2, here, :], factors[3, here, :], factors[4, here, :], wide[1]
        )


def add_kernel(own, received, out):
    out[...] = (own[...] + received[...].astype(F32)).astype(BF16)


def call(kernel, outs, args, scratch=(), name=None, spaces=()):
    whole = pl.BlockSpec(memory_space=pltpu.VMEM)
    spaces = list(spaces) + [pltpu.VMEM] * (len(args) - len(spaces))
    shapes = [jax.ShapeDtypeStruct(shape, dtype) for shape, dtype in outs]
    return pl.pallas_call(
        kernel,
        out_shape=shapes if len(shapes) > 1 else shapes[0],
        in_specs=[pl.BlockSpec(memory_space=space) for space in spaces],
        out_specs=[whole] * len(shapes) if len(shapes) > 1 else whole,
        scratch_shapes=scratch,
        compiler_params=pltpu.CompilerParams(vmem_limit_bytes=32 * 1024 * 1024),
        name=name,
    )(*args)


def from_partner(value, apart):
    pairs = [(source, source ^ apart) for source in range(lax.axis_size("narrow"))]
    return lax.ppermute(value, "narrow", pairs)


def body(
    charges,
    leaf_angle,
    lagrange,
    level_angle,
    level_self,
    level_peer,
    switch_angle,
    switch_matrix,
    out_angle,
    evaluate,
):
    square = (LANES, LANES)
    tile = pltpu.VMEM(square, F32)
    wide, narrow = lax.axis_size("wide"), lax.axis_size("narrow")
    packed, far_angle = call(
        pack_kernel,
        [((128 * PIECE, LANES), BF16), ((112, LANES), F32)],
        [pltpu.with_memory_space_constraint(x, pltpu.HBM) for x in (charges, leaf_angle, level_angle, out_angle)],
        [
            pltpu.VMEM((64, 2048), F32),
            pltpu.VMEM((64, LANES), F32),
            pltpu.VMEM((48, LANES), F32),
            pltpu.SemaphoreType.DMA((8,)),
        ],
        name="pack",
        spaces=[pltpu.HBM] * 4,
    )
    groups = [[w * narrow + r + side for w in range(wide) for side in range(2)] for r in range(0, narrow, 2)]
    packed = lax.all_to_all(
        packed.reshape(2 * wide, PIECE // 4, 4, LANES),
        ("wide", "narrow"),
        0,
        0,
        axis_index_groups=groups,
        tiled=True,
    ).reshape(128 * PIECE, LANES)
    far_angle = from_partner(far_angle, narrow // 2)
    parity = (lax.axis_index("narrow") & 1).astype(jnp.int32).reshape(1)
    source, tall, both, factors = call(
        target_kernel,
        [
            ((2 * LANES, 2 * LANES), BF16),
            ((2 * LANES, LANES), BF16),
            ((3, 2 * LANES, 2 * LANES), BF16),
            ((8, *square), F32),
        ],
        [parity, lagrange, level_angle, far_angle, switch_angle, out_angle, level_self, level_peer, switch_matrix, evaluate],
        [tile],
        name="target",
        spaces=[pltpu.SMEM],
    )
    middle, sent = call(
        switch_kernel,
        [((2048, LANES), F32), ((64, 2048), BF16)],
        [parity, packed, source, tall, both, factors],
        [pltpu.VMEM((2, 2048, LANES), F32), pltpu.VMEM((4, *square), F32)],
        name="switch",
        spaces=[pltpu.SMEM],
    )
    far = from_partner(sent, narrow // 2)
    own = call(last_kernel, [((64, 2048), F32)], [middle, both, factors], name="last")
    return call(add_kernel, [((64, 2048), BF16)], [own, far], name="add")


def solution(mesh):
    return jax.shard_map(
        body,
        mesh=mesh,
        in_specs=(
            P(None, ("wide", "narrow")),
            P(None, ("wide", "narrow")),
            P(),
            P(None, None, ("wide", "narrow")),
            P(),
            P(),
            P(None, ("wide", "narrow")),
            P(),
            P(None, ("wide", "narrow")),
            P(),
        ),
        out_specs=P(None, ("wide", "narrow")),
        check_vma=False,
    )
```

```python
import jax
import jax.numpy as jnp
from jax import lax
from jax.experimental import pallas as pl
from jax.experimental.pallas import tpu as pltpu
from jax.sharding import PartitionSpec as P

F32 = jnp.float32
BF16 = jnp.bfloat16
LANES = 128
CHUNK = 1024
WHOLE = 2048


def sin_cos(angle):
    turns = jnp.floor(angle * 0.6366197723675814 + 0.5)
    rest = angle - turns * 1.5703125
    rest = rest - turns * 4.837512969970703125e-4
    rest = rest - turns * 7.549789948768648e-8
    square = rest * rest
    sine = rest + rest * square * (
        -1.6666654611e-1 + square * (8.3321608736e-3 + square * -1.9515295891e-4)
    )
    cosine = (
        1.0
        - 0.5 * square
        + square
        * square
        * (4.166664568298827e-2 + square * (-1.388731625493765e-3 + square * 2.443315711809948e-5))
    )
    size = jnp.abs(turns)
    odd = size == 1.0
    sign = jnp.where(size == 2.0, -1.0, 1.0)
    return (
        jnp.where(odd, turns * cosine, sign * sine),
        jnp.where(odd, -turns * sine, sign * cosine),
    )


def halves(value):
    high = value.astype(BF16)
    return high, (value - high.astype(F32)).astype(BF16)


def dot(left, right):
    return jnp.dot(left, right, preferred_element_type=F32)


def wide_weights(matrix):
    high, low = halves(matrix)
    return jnp.concatenate(
        [jnp.concatenate([high, low], axis=1), jnp.concatenate([high, jnp.zeros_like(low)], axis=1)], axis=0
    )


def tall_weights(matrix):
    return jnp.concatenate(halves(matrix), axis=0)


def dot_exact(value, weights):
    return dot(jnp.concatenate([value, value], axis=1), weights)


def dot_wide(value, weights):
    both = dot(jnp.concatenate(halves(value), axis=1), weights)
    return both[:, :LANES] + both[:, LANES:]


def dot_full(left, right, dims=((1,), (0,))):
    return lax.dot_general(
        left, right, (dims, ((), ())), precision=lax.Precision.HIGHEST, preferred_element_type=F32
    )


def spread(rows, scratch):
    scratch[...] = jnp.zeros((LANES, LANES), F32)
    for to_row, from_row in ((0, 0), (64, 48)):
        for to_lane, from_lane in ((0, 0), (64, 48)):
            scratch[to_row : to_row + 48, to_lane : to_lane + 48] = rows[
                from_row : from_row + 48, from_lane : from_lane + 48
            ]
    return scratch[...]


def two_blocks(block, scratch):
    scratch[...] = jnp.zeros((LANES, LANES), F32)
    scratch[0:48, 0:64] = block
    scratch[64:112, 64:128] = block
    return scratch[...]


def rotation_factors(angle):
    sine, cosine = sin_cos(angle)
    gap = jnp.zeros((16, LANES), F32)
    cos_rows = jnp.concatenate([cosine, gap, cosine, gap], axis=0)
    sin_rows = jnp.concatenate([-sine, gap, sine, gap], axis=0)
    return cos_rows.T, sin_rows.T


def per_box(value, factor):
    boxes = factor.shape[0]
    return (value.reshape(boxes, 16, LANES) * factor[:, None, :]).reshape(boxes * 16, LANES)


def rotated(value, cos_factor, sin_factor):
    return per_box(value, cos_factor) + per_box(pltpu.roll(value, 64, 1), sin_factor)


GROUP = 4
PIECE = 20


def piece_rows(backward):
    pieces = lax.broadcasted_iota(jnp.int32, (8 * PIECE, 8 * PIECE), 1 if backward else 0)
    rows = lax.broadcasted_iota(jnp.int32, (8 * PIECE, 8 * PIECE), 0 if backward else 1)
    place, row = pieces // PIECE, pieces % PIECE
    wide, side = place // 2, place % 2
    angle = row - 16
    found = jnp.where(row < 16, wide * 16 + row, 64 + (angle // 2) * 8 + wide * 2 + angle % 2)
    if backward:
        return (rows == side * 80 + found).astype(F32).astype(BF16)
    return (rows == found).astype(F32).astype(BF16)[:, :80]


def angle_rows(angle):
    high = angle.astype(BF16).astype(F32)
    low = angle - high
    if angle.shape[0] == 64:
        return jnp.concatenate([high, low], axis=0).T
    gap = jnp.zeros((16, LANES), F32)
    return jnp.concatenate([high, gap, low, gap], axis=0).T


def pack_kernel(charges, leaf_angle, level_angle, out_angle, out, far_angle, held, angle, first_angle, sems):
    width = 512
    copies = []
    for step in range(2048 // width):
        here = pl.ds(step * width, width)
        copies.append(pltpu.make_async_copy(charges.at[:, here], held.at[:, here], sems.at[step]))
    near = [
        pltpu.make_async_copy(leaf_angle, angle, sems.at[4]),
        pltpu.make_async_copy(level_angle.at[0], first_angle, sems.at[5]),
    ]
    far = [
        pltpu.make_async_copy(level_angle.at[1], far_angle.at[0:48], sems.at[6]),
        pltpu.make_async_copy(out_angle, far_angle.at[48:112], sems.at[7]),
    ]
    for copy in near + copies + far:
        copy.start()
    order = piece_rows(False)
    low_lane = lax.broadcasted_iota(jnp.int32, (64, LANES), 1) < 64
    for copy in near + copies + far:
        copy.wait()
    leaf_rows = angle_rows(angle[...])
    level_rows = angle_rows(first_angle[...])
    for pair in range(8):
        rows = []
        for tile in (2 * pair, 2 * pair + 1):
            points = held[:, tile * LANES : (tile + 1) * LANES]
            both = jnp.concatenate([points, points], axis=0).T.reshape(GROUP, 2, 16, LANES)
            merged = jnp.where(low_lane, both[:, 0].reshape(64, LANES), both[:, 1].reshape(64, LANES))
            boxes = slice(tile * 8, (tile + 1) * 8)
            rows.append(jnp.concatenate([merged, leaf_rows[boxes], level_rows[boxes]], axis=0).astype(BF16))
        rows = dot(order, jnp.concatenate(rows, axis=1)).astype(BF16)
        out[pair * 320 : pair * 320 + 160, :] = rows[:, :LANES]
        out[pair * 320 + 160 : pair * 320 + 320, :] = rows[:, LANES:]


def target_kernel(
    parity, lagrange, level_angle, peer_angle, switch_angle, out_angle, level_self, level_peer, switch_matrix, evaluate, source, tall, wide, factors, scratch
):
    leaf = two_blocks(lagrange[...], scratch)
    self_weights = dot_full(leaf, spread(level_self.at[0], scratch), ((0,), (1,)))
    peer_weights = dot_full(leaf, spread(level_peer.at[0], scratch), ((0,), (1,)))
    even = parity[0] == 0
    for place in range(2):
        near, far = (self_weights, peer_weights) if place == 0 else (peer_weights, self_weights)
        high, low = halves(jnp.where(even, near, far))
        source[place * LANES : (place + 1) * LANES, :] = jnp.concatenate([high, low], axis=1)
    tall[...] = tall_weights(spread(level_peer.at[1], scratch).T)
    wide[0] = wide_weights(spread(level_self.at[1], scratch).T)
    scratch[...] = jnp.zeros((LANES, LANES), F32)
    scratch[0:64, 0:48] = evaluate[...]
    scratch[64:128, 64:112] = evaluate[...]
    wide[1] = wide_weights(scratch[...].T)
    wide[2] = wide_weights(spread(switch_matrix, scratch).T)
    factors[0], factors[1] = rotation_factors(switch_angle[...])
    factors[2], factors[3] = rotation_factors(level_angle[1])
    sine, cosine = sin_cos(out_angle[...])
    factors[4] = jnp.concatenate([cosine, -sine], axis=0).T
    factors[5], factors[6] = rotation_factors(peer_angle[0:48])
    sine, cosine = sin_cos(peer_angle[48:112])
    factors[7] = jnp.concatenate([cosine, -sine], axis=0).T


def evaluated(value, cos_factor, sin_factor, out_factor, last_weights):
    value = rotated(value, cos_factor, sin_factor)
    value = dot_wide(value, last_weights)
    value = per_box(value, out_factor)
    tiles = []
    for tile in range(value.shape[0] // LANES):
        turned = value[tile * LANES : (tile + 1) * LANES, :].T
        tiles.append(turned[0:64] + turned[64:128])
    return jnp.concatenate(tiles, axis=1)


def switch_kernel(parity, received, source, tall, wide, factors, middle, sent, points, turns):
    order = piece_rows(True)
    low_lane = lax.broadcasted_iota(jnp.int32, (64, LANES), 1) < 64
    for group in range(16):
        if group % 2 == 0:
            pair = dot(order, jnp.concatenate([received[(group + i) * 160 : (group + i + 1) * 160, :] for i in range(2)], axis=1))
        rows = pair[:, :LANES] if group % 2 == 0 else pair[:, LANES:]
        for side in range(2):
            merged = rows[side * 80 : side * 80 + 64]
            exchanged = pltpu.roll(merged, 64, 1)
            boxes = [
                jnp.where(low_lane, merged, exchanged).reshape(GROUP, 1, 16, LANES),
                jnp.where(low_lane, exchanged, merged).reshape(GROUP, 1, 16, LANES),
            ]
            points[side, group * LANES : (group + 1) * LANES, :] = jnp.concatenate(boxes, axis=1).reshape(LANES, LANES)
            turns[side, group * 8 : (group + 1) * 8, :] = rows[side * 80 + 64 : side * 80 + 72]
            turns[2 + side, group * 8 : (group + 1) * 8, :] = rows[side * 80 + 72 : side * 80 + 80]
    first_half = lax.broadcasted_iota(jnp.int32, (LANES, LANES), 1) < 64
    for side in range(2):
        angle = turns[side] + pltpu.roll(turns[side], 64, 1)
        sine, cosine = sin_cos(angle)
        turns[side] = jnp.where(first_half, cosine, sine)
    angle = jnp.where(parity[0] == 0, turns[2], turns[3])
    sine, cosine = sin_cos(angle + pltpu.roll(angle, 64, 1))
    turns[2] = cosine
    turns[3] = jnp.where(first_half, -sine, sine)
    boxes = WHOLE // 16
    for chunk in range(2048 // WHOLE):
        here = pl.ds(chunk * boxes, boxes)
        there = pl.ds(chunk * WHOLE, WHOLE)
        parts = [per_box(points[side, there, :], turns[side, here, :]).astype(BF16) for side in range(2)]
        both = dot(jnp.concatenate(parts, axis=1), source[...])
        value = both[:, :LANES] + both[:, LANES:]
        value = rotated(value, turns[2, here, :], turns[3, here, :])
        value = dot_wide(value, wide[2])
        value = rotated(value, factors[0, here, :], factors[1, here, :])
        middle[there, :] = value
        value = dot_exact(value.astype(BF16), tall[...])
        value = evaluated(value, factors[5, here, :], factors[6, here, :], factors[7, here, :], wide[1])
        sent[:, there] = value.astype(BF16)


def last_kernel(middle, wide, factors, own):
    boxes = CHUNK // 16
    for chunk in range(2048 // CHUNK):
        value = dot_wide(middle[chunk * CHUNK : (chunk + 1) * CHUNK, :], wide[0])
        here = pl.ds(chunk * boxes, boxes)
        own[:, chunk * CHUNK : (chunk + 1) * CHUNK] = evaluated(
            value, factors[2, here, :], factors[3, here, :], factors[4, here, :], wide[1]
        )


def add_kernel(own, received, out):
    out[...] = (own[...] + received[...].astype(F32)).astype(BF16)


def call(kernel, outs, args, scratch=(), name=None, spaces=(), out_spaces=()):
    out_spaces = list(out_spaces) + [pltpu.VMEM] * (len(outs) - len(out_spaces))
    targets = [pl.BlockSpec(memory_space=space) for space in out_spaces]
    spaces = list(spaces) + [pltpu.VMEM] * (len(args) - len(spaces))
    shapes = [jax.ShapeDtypeStruct(shape, dtype) for shape, dtype in outs]
    return pl.pallas_call(
        kernel,
        out_shape=shapes if len(shapes) > 1 else shapes[0],
        in_specs=[pl.BlockSpec(memory_space=space) for space in spaces],
        out_specs=targets if len(shapes) > 1 else targets[0],
        scratch_shapes=scratch,
        compiler_params=pltpu.CompilerParams(vmem_limit_bytes=32 * 1024 * 1024),
        name=name,
    )(*args)


def from_partner(value, apart):
    pairs = [(source, source ^ apart) for source in range(lax.axis_size("narrow"))]
    return lax.ppermute(value, "narrow", pairs)


def body(
    charges,
    leaf_angle,
    lagrange,
    level_angle,
    level_self,
    level_peer,
    switch_angle,
    switch_matrix,
    out_angle,
    evaluate,
):
    square = (LANES, LANES)
    tile = pltpu.VMEM(square, F32)
    wide, narrow = lax.axis_size("wide"), lax.axis_size("narrow")
    packed, far_angle = call(
        pack_kernel,
        [((128 * PIECE, LANES), BF16), ((112, LANES), F32)],
        [pltpu.with_memory_space_constraint(x, pltpu.HBM) for x in (charges, leaf_angle, level_angle, out_angle)],
        [
            pltpu.VMEM((64, 2048), F32),
            pltpu.VMEM((64, LANES), F32),
            pltpu.VMEM((48, LANES), F32),
            pltpu.SemaphoreType.DMA((8,)),
        ],
        name="pack",
        spaces=[pltpu.HBM] * 4,
    )
    groups = [[w * narrow + r + side for w in range(wide) for side in range(2)] for r in range(0, narrow, 2)]
    packed = lax.all_to_all(
        packed.reshape(2 * wide, PIECE // 4, 4, LANES),
        ("wide", "narrow"),
        0,
        0,
        axis_index_groups=groups,
        tiled=True,
    ).reshape(128 * PIECE, LANES)
    far_angle = from_partner(far_angle, narrow // 2)
    parity = (lax.axis_index("narrow") & 1).astype(jnp.int32).reshape(1)
    source, tall, both, factors = call(
        target_kernel,
        [
            ((2 * LANES, 2 * LANES), BF16),
            ((2 * LANES, LANES), BF16),
            ((3, 2 * LANES, 2 * LANES), BF16),
            ((8, *square), F32),
        ],
        [parity, lagrange, level_angle, far_angle, switch_angle, out_angle, level_self, level_peer, switch_matrix, evaluate],
        [tile],
        name="target",
        spaces=[pltpu.SMEM],
    )
    middle, sent = call(
        switch_kernel,
        [((2048, LANES), F32), ((64, 2048), BF16)],
        [parity, packed, source, tall, both, factors],
        [pltpu.VMEM((2, 2048, LANES), F32), pltpu.VMEM((4, *square), F32)],
        name="switch",
        spaces=[pltpu.SMEM],
    )
    far = from_partner(sent, narrow // 2)
    own = call(last_kernel, [((64, 2048), F32)], [middle, both, factors], name="last")
    return call(add_kernel, [((64, 2048), BF16)], [own, far], name="add")


def solution(mesh):
    return jax.shard_map(
        body,
        mesh=mesh,
        in_specs=(
            P(None, ("wide", "narrow")),
            P(None, ("wide", "narrow")),
            P(),
            P(None, None, ("wide", "narrow")),
            P(),
            P(),
            P(None, ("wide", "narrow")),
            P(),
            P(None, ("wide", "narrow")),
            P(),
        ),
        out_specs=P(None, ("wide", "narrow")),
        check_vma=False,
    )
```

```python
import jax
import jax.numpy as jnp
from jax import lax
from jax.experimental import pallas as pl
from jax.experimental.pallas import tpu as pltpu
from jax.sharding import PartitionSpec as P

F32 = jnp.float32
BF16 = jnp.bfloat16
LANES = 128
CHUNK = 1024
WHOLE = 2048


def sin_cos(angle):
    turns = jnp.floor(angle * 0.6366197723675814 + 0.5)
    rest = angle - turns * 1.5703125
    rest = rest - turns * 4.837512969970703125e-4
    rest = rest - turns * 7.549789948768648e-8
    square = rest * rest
    sine = rest + rest * square * (
        -1.6666654611e-1 + square * (8.3321608736e-3 + square * -1.9515295891e-4)
    )
    cosine = (
        1.0
        - 0.5 * square
        + square
        * square
        * (4.166664568298827e-2 + square * (-1.388731625493765e-3 + square * 2.443315711809948e-5))
    )
    size = jnp.abs(turns)
    odd = size == 1.0
    sign = jnp.where(size == 2.0, -1.0, 1.0)
    return (
        jnp.where(odd, turns * cosine, sign * sine),
        jnp.where(odd, -turns * sine, sign * cosine),
    )


def halves(value):
    high = value.astype(BF16)
    return high, (value - high.astype(F32)).astype(BF16)


def dot(left, right):
    return jnp.dot(left, right, preferred_element_type=F32)


def wide_weights(matrix):
    high, low = halves(matrix)
    return jnp.concatenate(
        [jnp.concatenate([high, low], axis=1), jnp.concatenate([high, jnp.zeros_like(low)], axis=1)], axis=0
    )


def tall_weights(matrix):
    return jnp.concatenate(halves(matrix), axis=0)


def dot_exact(value, weights):
    return dot(jnp.concatenate([value, value], axis=1), weights)


def dot_wide(value, weights):
    both = dot(jnp.concatenate(halves(value), axis=1), weights)
    return both[:, :LANES] + both[:, LANES:]


def dot_full(left, right, dims=((1,), (0,))):
    return lax.dot_general(
        left, right, (dims, ((), ())), precision=lax.Precision.HIGHEST, preferred_element_type=F32
    )


def spread(rows, scratch):
    scratch[...] = jnp.zeros((LANES, LANES), F32)
    for to_row, from_row in ((0, 0), (64, 48)):
        for to_lane, from_lane in ((0, 0), (64, 48)):
            scratch[to_row : to_row + 48, to_lane : to_lane + 48] = rows[
                from_row : from_row + 48, from_lane : from_lane + 48
            ]
    return scratch[...]


def two_blocks(block, scratch):
    scratch[...] = jnp.zeros((LANES, LANES), F32)
    scratch[0:48, 0:64] = block
    scratch[64:112, 64:128] = block
    return scratch[...]


def rotation_factors(angle):
    sine, cosine = sin_cos(angle)
    gap = jnp.zeros((16, LANES), F32)
    cos_rows = jnp.concatenate([cosine, gap, cosine, gap], axis=0)
    sin_rows = jnp.concatenate([-sine, gap, sine, gap], axis=0)
    return cos_rows.T, sin_rows.T


def per_box(value, factor):
    boxes = factor.shape[0]
    return (value.reshape(boxes, 16, LANES) * factor[:, None, :]).reshape(boxes * 16, LANES)


def rotated(value, cos_factor, sin_factor):
    return per_box(value, cos_factor) + per_box(pltpu.roll(value, 64, 1), sin_factor)


GROUP = 4
PIECE = 20


def piece_rows(backward):
    pieces = lax.broadcasted_iota(jnp.int32, (8 * PIECE, 8 * PIECE), 1 if backward else 0)
    rows = lax.broadcasted_iota(jnp.int32, (8 * PIECE, 8 * PIECE), 0 if backward else 1)
    place, row = pieces // PIECE, pieces % PIECE
    wide, side = place // 2, place % 2
    angle = row - 16
    found = jnp.where(row < 16, wide * 16 + row, 64 + (angle // 2) * 8 + wide * 2 + angle % 2)
    if backward:
        return (rows == side * 80 + found).astype(F32).astype(BF16)
    return (rows == found).astype(F32).astype(BF16)[:, :80]


def angle_rows(angle):
    high = angle.astype(BF16).astype(F32)
    low = angle - high
    if angle.shape[0] == 64:
        return jnp.concatenate([high, low], axis=0).T
    gap = jnp.zeros((16, LANES), F32)
    return jnp.concatenate([high, gap, low, gap], axis=0).T


def pack_kernel(charges, leaf_angle, level_angle, out_angle, out, far_angle, held, angle, first_angle, pieces, sems, sent):
    width = 512
    copies = []
    for step in range(2048 // width):
        here = pl.ds(step * width, width)
        copies.append(pltpu.make_async_copy(charges.at[:, here], held.at[:, here], sems.at[step]))
    near = [
        pltpu.make_async_copy(leaf_angle, angle, sems.at[4]),
        pltpu.make_async_copy(level_angle.at[0], first_angle, sems.at[5]),
    ]
    far = [
        pltpu.make_async_copy(level_angle.at[1], far_angle.at[0:48], sems.at[6]),
        pltpu.make_async_copy(out_angle, far_angle.at[48:112], sems.at[7]),
    ]
    for copy in near + copies + far:
        copy.start()
    order = piece_rows(False)
    low_lane = lax.broadcasted_iota(jnp.int32, (64, LANES), 1) < 64
    for copy in near + copies + far:
        copy.wait()
    leaf_rows = angle_rows(angle[...])
    level_rows = angle_rows(first_angle[...])
    writes = []
    for pair in range(8):
        rows = []
        for tile in (2 * pair, 2 * pair + 1):
            points = held[:, tile * LANES : (tile + 1) * LANES]
            both = jnp.concatenate([points, points], axis=0).T.reshape(GROUP, 2, 16, LANES)
            merged = jnp.where(low_lane, both[:, 0].reshape(64, LANES), both[:, 1].reshape(64, LANES))
            boxes = slice(tile * 8, (tile + 1) * 8)
            rows.append(jnp.concatenate([merged, leaf_rows[boxes], level_rows[boxes]], axis=0).astype(BF16))
        rows = dot(order, jnp.concatenate(rows, axis=1)).astype(BF16)
        pieces[pair * 320 : pair * 320 + 160, :] = rows[:, :LANES]
        pieces[pair * 320 + 160 : pair * 320 + 320, :] = rows[:, LANES:]
        if pair % 4 == 3:
            here = pl.ds((pair - 3) * 320, 1280)
            writes.append(pltpu.make_async_copy(pieces.at[here], out.at[here], sent.at[pair // 4]))
            writes[-1].start()
    for copy in writes:
        copy.wait()


def target_kernel(
    parity, lagrange, level_angle, peer_angle, switch_angle, out_angle, level_self, level_peer, switch_matrix, evaluate, source, tall, wide, factors, scratch
):
    leaf = two_blocks(lagrange[...], scratch)
    self_weights = dot_full(leaf, spread(level_self.at[0], scratch), ((0,), (1,)))
    peer_weights = dot_full(leaf, spread(level_peer.at[0], scratch), ((0,), (1,)))
    even = parity[0] == 0
    for place in range(2):
        near, far = (self_weights, peer_weights) if place == 0 else (peer_weights, self_weights)
        high, low = halves(jnp.where(even, near, far))
        source[place * LANES : (place + 1) * LANES, :] = jnp.concatenate([high, low], axis=1)
    tall[...] = tall_weights(spread(level_peer.at[1], scratch).T)
    wide[0] = wide_weights(spread(level_self.at[1], scratch).T)
    scratch[...] = jnp.zeros((LANES, LANES), F32)
    scratch[0:64, 0:48] = evaluate[...]
    scratch[64:128, 64:112] = evaluate[...]
    wide[1] = wide_weights(scratch[...].T)
    wide[2] = wide_weights(spread(switch_matrix, scratch).T)
    factors[0], factors[1] = rotation_factors(switch_angle[...])
    factors[2], factors[3] = rotation_factors(level_angle[1])
    sine, cosine = sin_cos(out_angle[...])
    factors[4] = jnp.concatenate([cosine, -sine], axis=0).T
    factors[5], factors[6] = rotation_factors(peer_angle[0:48])
    sine, cosine = sin_cos(peer_angle[48:112])
    factors[7] = jnp.concatenate([cosine, -sine], axis=0).T


def evaluated(value, cos_factor, sin_factor, out_factor, last_weights):
    value = rotated(value, cos_factor, sin_factor)
    value = dot_wide(value, last_weights)
    value = per_box(value, out_factor)
    tiles = []
    for tile in range(value.shape[0] // LANES):
        turned = value[tile * LANES : (tile + 1) * LANES, :].T
        tiles.append(turned[0:64] + turned[64:128])
    return jnp.concatenate(tiles, axis=1)


def switch_kernel(parity, received, source, tall, wide, factors, middle, sent, points, turns):
    order = piece_rows(True)
    low_lane = lax.broadcasted_iota(jnp.int32, (64, LANES), 1) < 64
    for group in range(16):
        if group % 2 == 0:
            pair = dot(order, jnp.concatenate([received[(group + i) * 160 : (group + i + 1) * 160, :] for i in range(2)], axis=1))
        rows = pair[:, :LANES] if group % 2 == 0 else pair[:, LANES:]
        for side in range(2):
            merged = rows[side * 80 : side * 80 + 64]
            exchanged = pltpu.roll(merged, 64, 1)
            boxes = [
                jnp.where(low_lane, merged, exchanged).reshape(GROUP, 1, 16, LANES),
                jnp.where(low_lane, exchanged, merged).reshape(GROUP, 1, 16, LANES),
            ]
            points[side, group * LANES : (group + 1) * LANES, :] = jnp.concatenate(boxes, axis=1).reshape(LANES, LANES)
            turns[side, group * 8 : (group + 1) * 8, :] = rows[side * 80 + 64 : side * 80 + 72]
            turns[2 + side, group * 8 : (group + 1) * 8, :] = rows[side * 80 + 72 : side * 80 + 80]
    first_half = lax.broadcasted_iota(jnp.int32, (LANES, LANES), 1) < 64
    for side in range(2):
        angle = turns[side] + pltpu.roll(turns[side], 64, 1)
        sine, cosine = sin_cos(angle)
        turns[side] = jnp.where(first_half, cosine, sine)
    angle = jnp.where(parity[0] == 0, turns[2], turns[3])
    sine, cosine = sin_cos(angle + pltpu.roll(angle, 64, 1))
    turns[2] = cosine
    turns[3] = jnp.where(first_half, -sine, sine)
    boxes = WHOLE // 16
    for chunk in range(2048 // WHOLE):
        here = pl.ds(chunk * boxes, boxes)
        there = pl.ds(chunk * WHOLE, WHOLE)
        parts = [per_box(points[side, there, :], turns[side, here, :]).astype(BF16) for side in range(2)]
        both = dot(jnp.concatenate(parts, axis=1), source[...])
        value = both[:, :LANES] + both[:, LANES:]
        value = rotated(value, turns[2, here, :], turns[3, here, :])
        value = dot_wide(value, wide[2])
        value = rotated(value, factors[0, here, :], factors[1, here, :])
        middle[there, :] = value
        value = dot_exact(value.astype(BF16), tall[...])
        value = evaluated(value, factors[5, here, :], factors[6, here, :], factors[7, here, :], wide[1])
        sent[:, there] = value.astype(BF16)


def last_kernel(middle, wide, factors, own):
    boxes = CHUNK // 16
    for chunk in range(2048 // CHUNK):
        value = dot_wide(middle[chunk * CHUNK : (chunk + 1) * CHUNK, :], wide[0])
        here = pl.ds(chunk * boxes, boxes)
        own[:, chunk * CHUNK : (chunk + 1) * CHUNK] = evaluated(
            value, factors[2, here, :], factors[3, here, :], factors[4, here, :], wide[1]
        )


def add_kernel(own, received, out):
    out[...] = (own[...] + received[...].astype(F32)).astype(BF16)


def call(kernel, outs, args, scratch=(), name=None, spaces=(), out_spaces=()):
    out_spaces = list(out_spaces) + [pltpu.VMEM] * (len(outs) - len(out_spaces))
    targets = [pl.BlockSpec(memory_space=space) for space in out_spaces]
    spaces = list(spaces) + [pltpu.VMEM] * (len(args) - len(spaces))
    shapes = [jax.ShapeDtypeStruct(shape, dtype) for shape, dtype in outs]
    return pl.pallas_call(
        kernel,
        out_shape=shapes if len(shapes) > 1 else shapes[0],
        in_specs=[pl.BlockSpec(memory_space=space) for space in spaces],
        out_specs=targets if len(shapes) > 1 else targets[0],
        scratch_shapes=scratch,
        compiler_params=pltpu.CompilerParams(vmem_limit_bytes=32 * 1024 * 1024),
        name=name,
    )(*args)


def from_partner(value, apart):
    pairs = [(source, source ^ apart) for source in range(lax.axis_size("narrow"))]
    return lax.ppermute(value, "narrow", pairs)


def body(
    charges,
    leaf_angle,
    lagrange,
    level_angle,
    level_self,
    level_peer,
    switch_angle,
    switch_matrix,
    out_angle,
    evaluate,
):
    square = (LANES, LANES)
    tile = pltpu.VMEM(square, F32)
    wide, narrow = lax.axis_size("wide"), lax.axis_size("narrow")
    packed, far_angle = call(
        pack_kernel,
        [((128 * PIECE, LANES), BF16), ((112, LANES), F32)],
        [pltpu.with_memory_space_constraint(x, pltpu.HBM) for x in (charges, leaf_angle, level_angle, out_angle)],
        [
            pltpu.VMEM((64, 2048), F32),
            pltpu.VMEM((64, LANES), F32),
            pltpu.VMEM((48, LANES), F32),
            pltpu.VMEM((128 * PIECE, LANES), BF16),
            pltpu.SemaphoreType.DMA((8,)),
            pltpu.SemaphoreType.DMA((2,)),
        ],
        name="pack",
        spaces=[pltpu.HBM] * 4,
        out_spaces=[pltpu.HBM],
    )
    groups = [[w * narrow + r + side for w in range(wide) for side in range(2)] for r in range(0, narrow, 2)]
    packed = lax.all_to_all(
        packed.reshape(2 * wide, PIECE // 4, 4, LANES),
        ("wide", "narrow"),
        0,
        0,
        axis_index_groups=groups,
        tiled=True,
    ).reshape(128 * PIECE, LANES)
    far_angle = from_partner(far_angle, narrow // 2)
    parity = (lax.axis_index("narrow") & 1).astype(jnp.int32).reshape(1)
    source, tall, both, factors = call(
        target_kernel,
        [
            ((2 * LANES, 2 * LANES), BF16),
            ((2 * LANES, LANES), BF16),
            ((3, 2 * LANES, 2 * LANES), BF16),
            ((8, *square), F32),
        ],
        [parity, lagrange, level_angle, far_angle, switch_angle, out_angle, level_self, level_peer, switch_matrix, evaluate],
        [tile],
        name="target",
        spaces=[pltpu.SMEM],
    )
    middle, sent = call(
        switch_kernel,
        [((2048, LANES), F32), ((64, 2048), BF16)],
        [parity, packed, source, tall, both, factors],
        [pltpu.VMEM((2, 2048, LANES), F32), pltpu.VMEM((4, *square), F32)],
        name="switch",
        spaces=[pltpu.SMEM],
    )
    far = from_partner(sent, narrow // 2)
    own = call(last_kernel, [((64, 2048), F32)], [middle, both, factors], name="last")
    return call(add_kernel, [((64, 2048), BF16)], [own, far], name="add")


def solution(mesh):
    return jax.shard_map(
        body,
        mesh=mesh,
        in_specs=(
            P(None, ("wide", "narrow")),
            P(None, ("wide", "narrow")),
            P(),
            P(None, None, ("wide", "narrow")),
            P(),
            P(),
            P(None, ("wide", "narrow")),
            P(),
            P(None, ("wide", "narrow")),
            P(),
        ),
        out_specs=P(None, ("wide", "narrow")),
        check_vma=False,
    )
```

```python
import jax
import jax.numpy as jnp
from jax import lax
from jax.experimental import pallas as pl
from jax.experimental.pallas import tpu as pltpu
from jax.sharding import PartitionSpec as P

F32 = jnp.float32
BF16 = jnp.bfloat16
LANES = 128
CHUNK = 1024
WHOLE = 2048


def sin_cos(angle):
    turns = jnp.floor(angle * 0.6366197723675814 + 0.5)
    rest = angle - turns * 1.5703125
    rest = rest - turns * 4.837512969970703125e-4
    rest = rest - turns * 7.549789948768648e-8
    square = rest * rest
    sine = rest + rest * square * (
        -1.6666654611e-1 + square * (8.3321608736e-3 + square * -1.9515295891e-4)
    )
    cosine = (
        1.0
        - 0.5 * square
        + square
        * square
        * (4.166664568298827e-2 + square * (-1.388731625493765e-3 + square * 2.443315711809948e-5))
    )
    size = jnp.abs(turns)
    odd = size == 1.0
    sign = jnp.where(size == 2.0, -1.0, 1.0)
    return (
        jnp.where(odd, turns * cosine, sign * sine),
        jnp.where(odd, -turns * sine, sign * cosine),
    )


def halves(value):
    high = value.astype(BF16)
    return high, (value - high.astype(F32)).astype(BF16)


def dot(left, right):
    return jnp.dot(left, right, preferred_element_type=F32)


def wide_weights(matrix):
    high, low = halves(matrix)
    return jnp.concatenate(
        [jnp.concatenate([high, low], axis=1), jnp.concatenate([high, jnp.zeros_like(low)], axis=1)], axis=0
    )


def tall_weights(matrix):
    return jnp.concatenate(halves(matrix), axis=0)


def dot_exact(value, weights):
    return dot(jnp.concatenate([value, value], axis=1), weights)


def dot_wide(value, weights):
    both = dot(jnp.concatenate(halves(value), axis=1), weights)
    return both[:, :LANES] + both[:, LANES:]


def dot_full(left, right, dims=((1,), (0,))):
    return lax.dot_general(
        left, right, (dims, ((), ())), precision=lax.Precision.HIGHEST, preferred_element_type=F32
    )


def spread(rows, scratch):
    scratch[...] = jnp.zeros((LANES, LANES), F32)
    for to_row, from_row in ((0, 0), (64, 48)):
        for to_lane, from_lane in ((0, 0), (64, 48)):
            scratch[to_row : to_row + 48, to_lane : to_lane + 48] = rows[
                from_row : from_row + 48, from_lane : from_lane + 48
            ]
    return scratch[...]


def two_blocks(block, scratch):
    scratch[...] = jnp.zeros((LANES, LANES), F32)
    scratch[0:48, 0:64] = block
    scratch[64:112, 64:128] = block
    return scratch[...]


def rotation_factors(angle):
    sine, cosine = sin_cos(angle)
    gap = jnp.zeros((16, LANES), F32)
    cos_rows = jnp.concatenate([cosine, gap, cosine, gap], axis=0)
    sin_rows = jnp.concatenate([-sine, gap, sine, gap], axis=0)
    return cos_rows.T, sin_rows.T


def per_box(value, factor):
    boxes = factor.shape[0]
    return (value.reshape(boxes, 16, LANES) * factor[:, None, :]).reshape(boxes * 16, LANES)


def rotated(value, cos_factor, sin_factor):
    return per_box(value, cos_factor) + per_box(pltpu.roll(value, 64, 1), sin_factor)


GROUP = 4
PIECE = 20


def piece_rows(backward):
    pieces = lax.broadcasted_iota(jnp.int32, (8 * PIECE, 8 * PIECE), 1 if backward else 0)
    rows = lax.broadcasted_iota(jnp.int32, (8 * PIECE, 8 * PIECE), 0 if backward else 1)
    place, row = pieces // PIECE, pieces % PIECE
    wide, side = place // 2, place % 2
    angle = row - 16
    found = jnp.where(row < 16, wide * 16 + row, 64 + (angle // 2) * 8 + wide * 2 + angle % 2)
    if backward:
        return (rows == side * 80 + found).astype(F32).astype(BF16)
    return (rows == found).astype(F32).astype(BF16)[:, :80]


def angle_rows(angle):
    high = angle.astype(BF16).astype(F32)
    low = angle - high
    if angle.shape[0] == 64:
        return jnp.concatenate([high, low], axis=0).T
    gap = jnp.zeros((16, LANES), F32)
    return jnp.concatenate([high, gap, low, gap], axis=0).T


def pack_kernel(charges, leaf_angle, level_angle, out_angle, out, far_angle, held, angle, first_angle, pieces, sems, sent):
    width = 512
    copies = []
    for step in range(2048 // width):
        here = pl.ds(step * width, width)
        copies.append(pltpu.make_async_copy(charges.at[:, here], held.at[:, here], sems.at[step]))
    near = [
        pltpu.make_async_copy(leaf_angle, angle, sems.at[4]),
        pltpu.make_async_copy(level_angle.at[0], first_angle, sems.at[5]),
    ]
    far = [
        pltpu.make_async_copy(level_angle.at[1], far_angle.at[0:48], sems.at[6]),
        pltpu.make_async_copy(out_angle, far_angle.at[48:112], sems.at[7]),
    ]
    for copy in near + copies + far:
        copy.start()
    order = piece_rows(False)
    low_lane = lax.broadcasted_iota(jnp.int32, (64, LANES), 1) < 64
    for copy in near:
        copy.wait()
    leaf_rows = angle_rows(angle[...])
    level_rows = angle_rows(first_angle[...])
    writes = []
    for pair in range(8):
        if pair % 4 == 0:
            for copy in copies[pair // 2 : pair // 2 + 2]:
                copy.wait()
        rows = []
        for tile in (2 * pair, 2 * pair + 1):
            points = held[:, tile * LANES : (tile + 1) * LANES]
            both = jnp.concatenate([points, points], axis=0).T.reshape(GROUP, 2, 16, LANES)
            merged = jnp.where(low_lane, both[:, 0].reshape(64, LANES), both[:, 1].reshape(64, LANES))
            boxes = slice(tile * 8, (tile + 1) * 8)
            rows.append(jnp.concatenate([merged, leaf_rows[boxes], level_rows[boxes]], axis=0).astype(BF16))
        rows = dot(order, jnp.concatenate(rows, axis=1)).astype(BF16)
        pieces[pair * 320 : pair * 320 + 160, :] = rows[:, :LANES]
        pieces[pair * 320 + 160 : pair * 320 + 320, :] = rows[:, LANES:]
        if pair % 4 == 3:
            here = pl.ds((pair - 3) * 320, 1280)
            writes.append(pltpu.make_async_copy(pieces.at[here], out.at[here], sent.at[pair // 4]))
            writes[-1].start()
    for copy in writes + far:
        copy.wait()


def target_kernel(
    parity, lagrange, level_angle, peer_angle, switch_angle, out_angle, level_self, level_peer, switch_matrix, evaluate, source, tall, wide, factors, scratch
):
    leaf = two_blocks(lagrange[...], scratch)
    self_weights = dot_full(leaf, spread(level_self.at[0], scratch), ((0,), (1,)))
    peer_weights = dot_full(leaf, spread(level_peer.at[0], scratch), ((0,), (1,)))
    even = parity[0] == 0
    for place in range(2):
        near, far = (self_weights, peer_weights) if place == 0 else (peer_weights, self_weights)
        high, low = halves(jnp.where(even, near, far))
        source[place * LANES : (place + 1) * LANES, :] = jnp.concatenate([high, low], axis=1)
    tall[...] = tall_weights(spread(level_peer.at[1], scratch).T)
    wide[0] = wide_weights(spread(level_self.at[1], scratch).T)
    scratch[...] = jnp.zeros((LANES, LANES), F32)
    scratch[0:64, 0:48] = evaluate[...]
    scratch[64:128, 64:112] = evaluate[...]
    wide[1] = wide_weights(scratch[...].T)
    wide[2] = wide_weights(spread(switch_matrix, scratch).T)
    factors[0], factors[1] = rotation_factors(switch_angle[...])
    factors[2], factors[3] = rotation_factors(level_angle[1])
    sine, cosine = sin_cos(out_angle[...])
    factors[4] = jnp.concatenate([cosine, -sine], axis=0).T
    factors[5], factors[6] = rotation_factors(peer_angle[0:48])
    sine, cosine = sin_cos(peer_angle[48:112])
    factors[7] = jnp.concatenate([cosine, -sine], axis=0).T


def evaluated(value, cos_factor, sin_factor, out_factor, last_weights):
    value = rotated(value, cos_factor, sin_factor)
    value = dot_wide(value, last_weights)
    value = per_box(value, out_factor)
    tiles = []
    for tile in range(value.shape[0] // LANES):
        turned = value[tile * LANES : (tile + 1) * LANES, :].T
        tiles.append(turned[0:64] + turned[64:128])
    return jnp.concatenate(tiles, axis=1)


def switch_kernel(parity, received, source, tall, wide, factors, middle, sent, points, turns):
    order = piece_rows(True)
    low_lane = lax.broadcasted_iota(jnp.int32, (64, LANES), 1) < 64
    for group in range(16):
        if group % 2 == 0:
            pair = dot(order, jnp.concatenate([received[(group + i) * 160 : (group + i + 1) * 160, :] for i in range(2)], axis=1))
        rows = pair[:, :LANES] if group % 2 == 0 else pair[:, LANES:]
        for side in range(2):
            merged = rows[side * 80 : side * 80 + 64]
            exchanged = pltpu.roll(merged, 64, 1)
            boxes = [
                jnp.where(low_lane, merged, exchanged).reshape(GROUP, 1, 16, LANES),
                jnp.where(low_lane, exchanged, merged).reshape(GROUP, 1, 16, LANES),
            ]
            points[side, group * LANES : (group + 1) * LANES, :] = jnp.concatenate(boxes, axis=1).reshape(LANES, LANES)
            turns[side, group * 8 : (group + 1) * 8, :] = rows[side * 80 + 64 : side * 80 + 72]
            turns[2 + side, group * 8 : (group + 1) * 8, :] = rows[side * 80 + 72 : side * 80 + 80]
    first_half = lax.broadcasted_iota(jnp.int32, (LANES, LANES), 1) < 64
    for side in range(2):
        angle = turns[side] + pltpu.roll(turns[side], 64, 1)
        sine, cosine = sin_cos(angle)
        turns[side] = jnp.where(first_half, cosine, sine)
    angle = jnp.where(parity[0] == 0, turns[2], turns[3])
    sine, cosine = sin_cos(angle + pltpu.roll(angle, 64, 1))
    turns[2] = cosine
    turns[3] = jnp.where(first_half, -sine, sine)
    boxes = WHOLE // 16
    for chunk in range(2048 // WHOLE):
        here = pl.ds(chunk * boxes, boxes)
        there = pl.ds(chunk * WHOLE, WHOLE)
        parts = [per_box(points[side, there, :], turns[side, here, :]).astype(BF16) for side in range(2)]
        both = dot(jnp.concatenate(parts, axis=1), source[...])
        value = both[:, :LANES] + both[:, LANES:]
        value = rotated(value, turns[2, here, :], turns[3, here, :])
        value = dot_wide(value, wide[2])
        value = rotated(value, factors[0, here, :], factors[1, here, :])
        middle[there, :] = value
        value = dot_exact(value.astype(BF16), tall[...])
        value = evaluated(value, factors[5, here, :], factors[6, here, :], factors[7, here, :], wide[1])
        sent[:, there] = value.astype(BF16)


def last_kernel(middle, wide, factors, own):
    boxes = CHUNK // 16
    for chunk in range(2048 // CHUNK):
        value = dot_wide(middle[chunk * CHUNK : (chunk + 1) * CHUNK, :], wide[0])
        here = pl.ds(chunk * boxes, boxes)
        own[:, chunk * CHUNK : (chunk + 1) * CHUNK] = evaluated(
            value, factors[2, here, :], factors[3, here, :], factors[4, here, :], wide[1]
        )


def add_kernel(own, received, out):
    out[...] = (own[...] + received[...].astype(F32)).astype(BF16)


def call(kernel, outs, args, scratch=(), name=None, spaces=(), out_spaces=()):
    out_spaces = list(out_spaces) + [pltpu.VMEM] * (len(outs) - len(out_spaces))
    targets = [pl.BlockSpec(memory_space=space) for space in out_spaces]
    spaces = list(spaces) + [pltpu.VMEM] * (len(args) - len(spaces))
    shapes = [jax.ShapeDtypeStruct(shape, dtype) for shape, dtype in outs]
    return pl.pallas_call(
        kernel,
        out_shape=shapes if len(shapes) > 1 else shapes[0],
        in_specs=[pl.BlockSpec(memory_space=space) for space in spaces],
        out_specs=targets if len(shapes) > 1 else targets[0],
        scratch_shapes=scratch,
        compiler_params=pltpu.CompilerParams(vmem_limit_bytes=32 * 1024 * 1024),
        name=name,
    )(*args)


def from_partner(value, apart):
    pairs = [(source, source ^ apart) for source in range(lax.axis_size("narrow"))]
    return lax.ppermute(value, "narrow", pairs)


def body(
    charges,
    leaf_angle,
    lagrange,
    level_angle,
    level_self,
    level_peer,
    switch_angle,
    switch_matrix,
    out_angle,
    evaluate,
):
    square = (LANES, LANES)
    tile = pltpu.VMEM(square, F32)
    wide, narrow = lax.axis_size("wide"), lax.axis_size("narrow")
    packed, far_angle = call(
        pack_kernel,
        [((128 * PIECE, LANES), BF16), ((112, LANES), F32)],
        [pltpu.with_memory_space_constraint(x, pltpu.HBM) for x in (charges, leaf_angle, level_angle, out_angle)],
        [
            pltpu.VMEM((64, 2048), F32),
            pltpu.VMEM((64, LANES), F32),
            pltpu.VMEM((48, LANES), F32),
            pltpu.VMEM((128 * PIECE, LANES), BF16),
            pltpu.SemaphoreType.DMA((8,)),
            pltpu.SemaphoreType.DMA((2,)),
        ],
        name="pack",
        spaces=[pltpu.HBM] * 4,
        out_spaces=[pltpu.HBM],
    )
    groups = [[w * narrow + r + side for w in range(wide) for side in range(2)] for r in range(0, narrow, 2)]
    packed = lax.all_to_all(
        packed.reshape(2 * wide, PIECE // 4, 4, LANES),
        ("wide", "narrow"),
        0,
        0,
        axis_index_groups=groups,
        tiled=True,
    ).reshape(128 * PIECE, LANES)
    far_angle = from_partner(far_angle, narrow // 2)
    parity = (lax.axis_index("narrow") & 1).astype(jnp.int32).reshape(1)
    source, tall, both, factors = call(
        target_kernel,
        [
            ((2 * LANES, 2 * LANES), BF16),
            ((2 * LANES, LANES), BF16),
            ((3, 2 * LANES, 2 * LANES), BF16),
            ((8, *square), F32),
        ],
        [parity, lagrange, level_angle, far_angle, switch_angle, out_angle, level_self, level_peer, switch_matrix, evaluate],
        [tile],
        name="target",
        spaces=[pltpu.SMEM],
    )
    middle, sent = call(
        switch_kernel,
        [((2048, LANES), F32), ((64, 2048), BF16)],
        [parity, packed, source, tall, both, factors],
        [pltpu.VMEM((2, 2048, LANES), F32), pltpu.VMEM((4, *square), F32)],
        name="switch",
        spaces=[pltpu.SMEM],
    )
    far = from_partner(sent, narrow // 2)
    own = call(last_kernel, [((64, 2048), F32)], [middle, both, factors], name="last")
    return call(add_kernel, [((64, 2048), BF16)], [own, far], name="add")


def solution(mesh):
    return jax.shard_map(
        body,
        mesh=mesh,
        in_specs=(
            P(None, ("wide", "narrow")),
            P(None, ("wide", "narrow")),
            P(),
            P(None, None, ("wide", "narrow")),
            P(),
            P(),
            P(None, ("wide", "narrow")),
            P(),
            P(None, ("wide", "narrow")),
            P(),
        ),
        out_specs=P(None, ("wide", "narrow")),
        check_vma=False,
    )
```
